32 devices in a mesh: chan: 8 (over z, core), win: 4 (over y, x).
Axes of the slice: x: 2, y: 2, z: 4, core: 2. Of those that a mesh axis runs over, the one named last changes fastest.
Arguments:
- traces: bfloat16 [4, 1024, 768], P('win', 'chan')
- pairing: int32 [2, 8], replicated, may hold values from 0 to 7, as said below
- aux_owners: int32 [1], replicated, may hold values from 0 to 7
- coda_start: int32 [1, 128], replicated, may hold values from 0 to 31
- coda_end: int32 [1, 128], replicated, may hold values from 96 to 128
Outputs:
- pair_coherence: bfloat16 [2, 1024, 256, 128], P(None, 'chan', 'win')
- coda_coherence: bfloat16 [1024, 128, 128], P('chan', 'win')
The draws below stay inside these ranges and needn't reach their ends.
Inputs may be any that keep to these rules, and one draw needn't show every extreme that they name: `pairing`: each row is a round of a round-robin plan: it pairs every block with another block, and the block's partner names it back; the rows are different rounds.
All inputs are finite; a program needn't handle non-finite values.
Results may differ from the reference program's by a relative error of at most 0.0075.
Values may be sent and summed in bfloat16 or wider, within the bound.
No kernel may reach another device: no remote copies, remote signals or barrier semaphores. Data moves between devices by JAX's collectives and lax.ppermute only.
A program may use at most 384 MiB of HBM per device.

```python
import math
import jax
import jax.numpy as jnp
from jax import lax

BLK = 128
LAGS = 256
CODA = 128
CODA_LO = 128
LAGS3 = 128
ROUNDS = 2
AUX = 1
WLEN = 768
W_DEV = 1
WINDOWS = 4
CHANNELS = 1024
N_CHAN = 8
N_WIN = 4


def draw_traces(key, part):
    key_noise, key_scale = jax.random.split(key)
    shape = (WINDOWS, CHANNELS, WLEN)
    noise = jax.random.normal(key_noise, shape, jnp.float32)
    scales = jnp.exp(jax.random.uniform(key_scale, (WINDOWS, CHANNELS, 1), jnp.float32, 0.0, jnp.log(10.0)))
    return (noise * scales).astype(jnp.bfloat16)


def draw_pairing(key, part):
    key_order, key_rounds = jax.random.split(jax.random.fold_in(key, 7))
    order = jax.random.permutation(key_order, N_CHAN).astype(jnp.int32)
    chosen = jax.random.permutation(key_rounds, N_CHAN - 1).astype(jnp.int32)[:ROUNDS]
    positions = jnp.arange(N_CHAN, dtype=jnp.int32)

    def one_round(round_value):
        mate = jnp.mod(2 * round_value - positions, N_CHAN - 1)
        mate = jnp.where(mate == positions, N_CHAN - 1, mate)
        mate = jnp.where(positions == N_CHAN - 1, round_value, mate)
        return jnp.zeros((N_CHAN,), jnp.int32).at[order].set(order[mate])
    return jax.vmap(one_round)(chosen).astype(jnp.int32)


def place_ends(array, rng, least, high):
    longest = array.shape.index(max(array.shape))
    spots = []
    for shift in (0, 1):
        where = [jax.random.randint(jax.random.fold_in(rng, axis), (), 0, length) for axis, length in enumerate(array.shape)]
        where[longest] = (where[longest] + shift) % array.shape[longest]
        spots.append(tuple(where))
    return array.at[spots[0]].set(least).at[spots[1]].set(high)


def setup_inputs(seed: int = 0) -> dict:
    key_of = jax.random.split(jax.random.key(seed), 6)
    traces = draw_traces(jax.random.fold_in(key_of[5], 71), 0)
    pairing = draw_pairing(jax.random.fold_in(key_of[5], 71), 0)
    aux_owners = jax.random.randint(key_of[2], (AUX,), 0, N_CHAN).astype(jnp.int32)
    coda_start = place_ends(jax.random.randint(key_of[3], (AUX, BLK), 0, CODA // 4), jax.random.fold_in(key_of[3], 1), 0, (CODA // 4) - 1).astype(jnp.int32)
    coda_end = place_ends(jax.random.randint(key_of[4], (AUX, BLK), 3 * CODA // 4, CODA + 1), jax.random.fold_in(key_of[4], 1), 3 * CODA // 4, CODA).astype(jnp.int32)
    return dict(traces=traces, pairing=pairing, aux_owners=aux_owners, coda_start=coda_start, coda_end=coda_end)


EPS = 1e-05

def whiten(traces):
    samples = traces.astype(jnp.float32)
    energy_mean = lax.optimization_barrier(jnp.mean(samples * samples, axis=-1, keepdims=True))
    return (samples * lax.rsqrt(energy_mean + EPS)).astype(jnp.bfloat16)

def correlate(sources, receivers, lag_first, lag_count):
    length = receivers.shape[-1]
    padded = jnp.pad(receivers.astype(jnp.float32), ((0, 0), (0, 0), (0, 0), (0, lag_first + lag_count)))
    weights = sources.astype(jnp.float32)
    lag_group = math.gcd(lag_count, 32)
    pieces = []
    for offset in range(0, lag_count, lag_group):
        shifted = jnp.stack([lax.slice_in_dim(padded, lag_first + offset + lag_value, lag_first + offset + lag_value + length, axis=3) for lag_value in range(lag_group)])
        pieces.append(jnp.einsum('gwit,lgwjt->gilj', weights, shifted))
    return jnp.concatenate(pieces, axis=2)

def reference(traces, pairing, aux_owners, coda_start, coda_end):
    white = whiten(traces)
    scale_two = 1.0 / math.sqrt(WINDOWS * WLEN)
    scale_three = 1.0 / math.sqrt(AUX * BLK * CODA)
    blocked = white.reshape(WINDOWS, N_CHAN, BLK, WLEN)
    aux_groups = jnp.take(blocked, aux_owners, axis=1).reshape(N_WIN, W_DEV, AUX, BLK, WLEN)
    lag_axis = jnp.arange(CODA, dtype=jnp.int32)
    live = (lag_axis[None, None, :] >= coda_start[:, :, None]) & (lag_axis[None, None, :] < coda_end[:, :, None])

    def per_block(block_index):
        own_rows = lax.dynamic_index_in_dim(blocked, block_index, 1, keepdims=False)
        collected = []
        for round_index in range(ROUNDS):
            partner = jnp.take(blocked, pairing[round_index, block_index], axis=1)
            collected.append(correlate(own_rows[None], partner[None], 0, LAGS)[0])
        pair_rows = (jnp.stack(collected) * scale_two).astype(jnp.bfloat16)
        own_groups = own_rows.reshape(N_WIN, W_DEV, BLK, WLEN)
        totals = []
        for aux_index in range(AUX):
            partial_value = correlate(aux_groups[:, :, aux_index], own_groups, CODA_LO, CODA) * scale_two
            rounded = lax.optimization_barrier(partial_value.astype(jnp.bfloat16)).astype(jnp.float32)
            totals.append(lax.optimization_barrier(jnp.sum(rounded, axis=0)))
        summed = jnp.stack(totals)
        coda = jnp.where(live[:, :, :, None], summed, 0.0).astype(jnp.bfloat16)
        coda_wide = lax.optimization_barrier(coda).astype(jnp.float32)
        padded = jnp.pad(coda_wide, ((0, 0), (0, 0), (0, LAGS3), (0, 0)))
        lag_group = math.gcd(LAGS3, 8)
        pieces = []
        for offset in range(0, LAGS3, lag_group):
            shifted = jnp.stack([lax.slice_in_dim(padded, offset + lag_value, offset + lag_value + CODA, axis=2) for lag_value in range(lag_group)])
            pieces.append(jnp.einsum('ksti,lkstj->ilj', coda_wide, shifted))
        three_rows = (jnp.concatenate(pieces, axis=1) * scale_three).astype(jnp.bfloat16)
        return (pair_rows, three_rows)
    pair_rows, three_rows = lax.map(per_block, jnp.arange(N_CHAN, dtype=jnp.int32))
    pair_out = jnp.transpose(pair_rows, (1, 0, 2, 3, 4)).reshape(ROUNDS, CHANNELS, LAGS, BLK)
    three_out = three_rows.reshape(CHANNELS, LAGS3, BLK)
    return (pair_out, three_out)
```

```python
import functools
import math

import jax
import jax.numpy as jnp
from jax import lax
from jax.experimental import pallas as pl
from jax.experimental.pallas import tpu as pltpu
from jax.sharding import PartitionSpec as P

LAGS = 256
CODA = 128
CODA_LO = 128
LAGS3 = 128
EPS = 1e-05
STEP = 16
GROUP = 4
VMEM_LIMIT = 60 << 20

f32 = jnp.float32
bf16 = jnp.bfloat16


def whiten(traces):
    samples = traces.astype(f32)
    energy_mean = jnp.mean(samples * samples, axis=-1, keepdims=True)
    return (samples * lax.rsqrt(energy_mean + EPS)).astype(bf16)


def shift_right(block, count):
    if count == 0:
        return block.astype(bf16)
    moved = pltpu.roll(block, count, 1)
    lane = lax.broadcasted_iota(jnp.int32, block.shape, 1)
    return jnp.where(lane < count, 0.0, moved).astype(bf16)


def coda_kernel(win_ref, aux_ref, own_ref, start_ref, end_ref, out_ref, shifted, own_t, coda, coda_t, acc, rows):
    windows, blk, length = own_ref.shape
    used = length - CODA_LO
    share = out_ref.shape[1]
    steps = share // 2
    pairs = CODA // 2
    scale_two = 1.0 / math.sqrt(windows * length)
    scale_three = 1.0 / math.sqrt(blk * CODA)
    win = win_ref[0]

    for w in range(windows):
        own_t[w, :length, :] = own_ref[w].T
        own_t[w, length:, :] = jnp.zeros((own_t.shape[1] - length, blk), bf16)
        samples = aux_ref[w][:, :used].astype(f32)
        for b in range(STEP):
            shifted[b * blk : (b + 1) * blk, w * used : (w + 1) * used] = shift_right(samples, b)
    coda[CODA * blk :, :] = jnp.zeros((coda.shape[0] - CODA * blk, blk), bf16)
    coda_t[: (steps - 1) * blk, :] = jnp.zeros(((steps - 1) * blk, 2 * blk), bf16)

    half = STEP // 2

    def part(step, _):
        a_pair = step // 2
        b_half = step % 2
        pieces = []
        for w in range(windows):
            halves = [
                own_t[w, pl.ds(pl.multiple_of(CODA_LO + (2 * a_pair + a) * STEP, STEP), used), :]
                for a in range(2)
            ]
            pieces.append(jnp.concatenate(halves, axis=1))
        weights = jnp.concatenate(pieces, axis=0)
        first = pl.multiple_of(b_half * half * blk, blk)
        result = jnp.dot(shifted[pl.ds(first, half * blk), :], weights, preferred_element_type=f32)
        for b in range(half):
            for a in range(2):
                lag = (2 * a_pair + a) * STEP + b_half * half + b
                tile = result[b * blk : (b + 1) * blk, a * blk : (a + 1) * blk] * scale_two
                live = (lag >= start_ref[...]) & (lag < end_ref[...])
                tile = jnp.where(live, tile, 0.0)
                coda[pl.ds(pl.multiple_of(lag * blk, blk), blk), :] = tile.astype(bf16)
                row = pl.multiple_of((lag // 2 + steps - 1) * blk, blk)
                coda_t[pl.ds(row, blk), (b % 2) * blk : (b % 2 + 1) * blk] = tile.T.astype(bf16)
        return 0

    lax.fori_loop(0, CODA // STEP, part, 0)

    acc[...] = jnp.zeros(acc.shape, f32)

    def accumulate(group, blocks):
        lhs, rhs = [], []
        for q in range(GROUP):
            pair = group * GROUP + q
            row = (pair + steps - blocks) * blk
            lhs.append(coda_t[pl.ds(pl.multiple_of(row, blk), blocks * blk), :])
            first = (2 * pair + win * share) * blk
            rhs.append(
                jnp.concatenate(
                    [coda[pl.ds(pl.multiple_of(first + b * blk, blk), 2 * blk), :] for b in range(2)], axis=1
                )
            )
        value = jnp.dot(
            jnp.concatenate(lhs, axis=1), jnp.concatenate(rhs, axis=0), preferred_element_type=f32
        )
        acc[(steps - blocks) * blk :, :] += value

    peeled = steps // GROUP - 1
    for group in range(peeled):
        accumulate(group, (group + 1) * GROUP)
    groups = pairs // GROUP - win * (share // (2 * GROUP))

    def whole(group, _):
        accumulate(group, steps)
        return 0

    lax.fori_loop(peeled, groups, whole, 0)
    for i in range(steps):
        for b in range(2):
            lag = 2 * (steps - 1 - i) + b
            rows[pl.ds(lag, blk, stride=share), :] = (
                acc[i * blk : (i + 1) * blk, b * blk : (b + 1) * blk] * scale_three
            )
    out_ref[...] = rows[...].reshape(blk, share, blk).astype(bf16)


def pair_kernel(win_ref, own_ref, partner_ref, out_ref, shifted, partner_t, rows):
    windows, blk, length = own_ref.shape
    rounds = partner_ref.shape[1]
    share = out_ref.shape[2]
    scale_two = 1.0 / math.sqrt(windows * length)
    win = win_ref[0]
    for w in range(windows):
        for r in range(rounds):
            partner_t[w, :length, r * blk : (r + 1) * blk] = partner_ref[w, r].T
        partner_t[w, length:, :] = jnp.zeros((partner_t.shape[1] - length, rounds * blk), bf16)
        samples = own_ref[w].astype(f32)
        for b in range(STEP):
            shifted[b * blk : (b + 1) * blk, w * length : (w + 1) * length] = shift_right(samples, b)

    half = STEP // 2

    def pair(step, _):
        a = step // 2
        b_half = step % 2
        first = pl.multiple_of(win * share + a * STEP, STEP)
        weights = jnp.concatenate([partner_t[w, pl.ds(first, length), :] for w in range(windows)], axis=0)
        row = pl.multiple_of(b_half * half * blk, blk)
        result = jnp.dot(shifted[pl.ds(row, half * blk), :], weights, preferred_element_type=f32)
        for b in range(half):
            lag = a * STEP + b_half * half + b
            for r in range(rounds):
                rows[r, pl.ds(lag, blk, stride=share), :] = (
                    result[b * blk : (b + 1) * blk, r * blk : (r + 1) * blk] * scale_two
                )
        return 0

    lax.fori_loop(0, 2 * (share // STEP), pair, 0)
    for r in range(rounds):
        out_ref[r] = rows[r].reshape(blk, share, blk).astype(bf16)


SMEM_SPEC = pl.BlockSpec(memory_space=pltpu.SMEM)
VMEM_SPEC = pl.BlockSpec(memory_space=pltpu.VMEM)


def coda_coherence(win, aux, own, start, end, share):
    windows, blk, length = own.shape
    used = length - CODA_LO
    steps = share // 2
    return pl.pallas_call(
        coda_kernel,
        out_shape=jax.ShapeDtypeStruct((blk, share, blk), bf16),
        in_specs=[SMEM_SPEC] + [VMEM_SPEC] * 4,
        out_specs=VMEM_SPEC,
        scratch_shapes=[
            pltpu.VMEM((STEP * blk, windows * used), bf16),
            pltpu.VMEM((windows, length + CODA, blk), bf16),
            pltpu.VMEM(((CODA + 1) * blk, blk), bf16),
            pltpu.VMEM(((CODA // 2 + steps - 1) * blk, 2 * blk), bf16),
            pltpu.VMEM((steps * blk, 2 * blk), f32),
            pltpu.VMEM((share * blk, blk), f32),
        ],
        compiler_params=pltpu.CompilerParams(vmem_limit_bytes=VMEM_LIMIT),
        name="coda_coherence",
    )(win, aux, own, start, end)


def pair_coherence(win, own, partner, share):
    windows, blk, length = own.shape
    rounds = partner.shape[1]
    return pl.pallas_call(
        pair_kernel,
        out_shape=jax.ShapeDtypeStruct((rounds, blk, share, blk), bf16),
        in_specs=[SMEM_SPEC] + [VMEM_SPEC] * 2,
        out_specs=VMEM_SPEC,
        scratch_shapes=[
            pltpu.VMEM((STEP * blk, windows * length), bf16),
            pltpu.VMEM((windows, length + LAGS, rounds * blk), bf16),
            pltpu.VMEM((rounds, blk * share, blk), f32),
        ],
        compiler_params=pltpu.CompilerParams(vmem_limit_bytes=VMEM_LIMIT),
        name="pair_coherence",
    )(win, own, partner)


def per_device(traces, pairing, aux_owners, coda_start, coda_end):
    win_size = lax.axis_size("win")
    chan_size = lax.axis_size("chan")
    win_index = lax.axis_index("win")
    chan_index = lax.axis_index("chan")
    blk = traces.shape[1]
    white = whiten(traces)[0]

    def exchange(block, k):
        return lax.ppermute(block, "win", [(i, i ^ k) for i in range(win_size)])

    own_all = jnp.stack([white] + [exchange(white, k) for k in range(1, win_size)])
    same_core = [list(range(core, chan_size, 2)) for core in range(2)]
    column = lax.all_gather(white, "chan", axis=0, axis_index_groups=same_core)
    other = lax.ppermute(column, "chan", [(i, i ^ 1) for i in range(chan_size)])
    both = jnp.stack([column, other])

    def pick(block):
        return both[(block % 2) ^ (chan_index % 2), block // 2]

    aux = pick(aux_owners[0])
    partners = jnp.stack([pick(pairing[r, chan_index]) for r in range(pairing.shape[0])])
    aux_all = jnp.stack([aux] + [exchange(aux, k) for k in range(1, win_size)])
    partner_all = jnp.stack([partners] + [exchange(partners, k) for k in range(1, win_size)])
    win = win_index.reshape(1).astype(jnp.int32)
    start = jnp.broadcast_to(coda_start[0][:, None], (blk, blk))
    end = jnp.broadcast_to(coda_end[0][:, None], (blk, blk))
    three = coda_coherence(win, aux_all, own_all, start, end, LAGS3 // win_size)
    pair = pair_coherence(win, own_all, partner_all, LAGS // win_size)
    return (pair, three)


def solution(mesh):
    in_specs = (P("win", "chan", None), P(), P(), P(), P())
    out_specs = (P(None, "chan", "win", None), P("chan", "win", None))
    return jax.shard_map(per_device, mesh=mesh, in_specs=in_specs, out_specs=out_specs, check_vma=False)
```

```python
import functools
import math

import jax
import jax.numpy as jnp
from jax import lax
from jax.experimental import pallas as pl
from jax.experimental.pallas import tpu as pltpu
from jax.sharding import PartitionSpec as P

LAGS = 256
CODA = 128
CODA_LO = 128
LAGS3 = 128
EPS = 1e-05
STEP = 16
GROUP = 4
VMEM_LIMIT = 60 << 20

SMEM_SPEC = pl.BlockSpec(memory_space=pltpu.SMEM)
VMEM_SPEC = pl.BlockSpec(memory_space=pltpu.VMEM)
ROW_PAD = 8

f32 = jnp.float32
bf16 = jnp.bfloat16


def whiten_kernel(traces_ref, out_ref):
    samples = traces_ref[0].astype(f32)
    energy_mean = jnp.mean(samples * samples, axis=-1, keepdims=True)
    out_ref[...] = (samples * lax.rsqrt(energy_mean + EPS)).astype(bf16)


def whiten(traces):
    return pl.pallas_call(
        whiten_kernel,
        out_shape=jax.ShapeDtypeStruct(traces.shape[1:], bf16),
        in_specs=[VMEM_SPEC],
        out_specs=VMEM_SPEC,
        name="whiten",
    )(traces)


def shift_right(block, count):
    if count == 0:
        return block.astype(bf16)
    moved = pltpu.roll(block, count, 1)
    lane = lax.broadcasted_iota(jnp.int32, block.shape, 1)
    return jnp.where(lane < count, 0.0, moved).astype(bf16)


def coda_kernel(windows, win_ref, start_ref, end_ref, *refs):
    aux_ref, own_ref = refs[:windows], refs[windows : 2 * windows]
    out_ref, shifted, own_t, coda, coda_t, acc, rows = refs[2 * windows :]
    blk, length = own_ref[0].shape
    used = length - CODA_LO
    share = out_ref.shape[1]
    steps = share // 2
    pairs = CODA // 2
    scale_two = 1.0 / math.sqrt(windows * length)
    scale_three = 1.0 / math.sqrt(blk * CODA)
    win = win_ref[0]

    for w in range(windows):
        own_t[w, :length, :] = own_ref[w][...].T
        own_t[w, length:, :] = jnp.zeros((own_t.shape[1] - length, blk), bf16)
        samples = aux_ref[w][:, :used].astype(f32)
        for b in range(STEP):
            shifted[b * blk : (b + 1) * blk, w * used : (w + 1) * used] = shift_right(samples, b)
    coda[CODA * blk :, :] = jnp.zeros((coda.shape[0] - CODA * blk, blk), bf16)
    coda_t[: (steps - 1) * blk, :] = jnp.zeros(((steps - 1) * blk, 2 * blk), bf16)

    half = STEP // 2

    def part(step, _):
        a_pair = step // 2
        b_half = step % 2
        pieces = []
        for w in range(windows):
            halves = [
                own_t[w, pl.ds(pl.multiple_of(CODA_LO + (2 * a_pair + a) * STEP, STEP), used), :]
                for a in range(2)
            ]
            pieces.append(jnp.concatenate(halves, axis=1))
        weights = jnp.concatenate(pieces, axis=0)
        first = pl.multiple_of(b_half * half * blk, blk)
        result = jnp.dot(shifted[pl.ds(first, half * blk), :], weights, preferred_element_type=f32)
        for b in range(half):
            for a in range(2):
                lag = (2 * a_pair + a) * STEP + b_half * half + b
                tile = result[b * blk : (b + 1) * blk, a * blk : (a + 1) * blk] * scale_two
                live = (lag >= start_ref[...]) & (lag < end_ref[...])
                tile = jnp.where(live, tile, 0.0)
                coda[pl.ds(pl.multiple_of(lag * blk, blk), blk), :] = tile.astype(bf16)
                row = pl.multiple_of((lag // 2 + steps - 1) * blk, blk)
                coda_t[pl.ds(row, blk), (b % 2) * blk : (b % 2 + 1) * blk] = tile.T.astype(bf16)
        return 0

    lax.fori_loop(0, CODA // STEP, part, 0)

    acc[...] = jnp.zeros(acc.shape, f32)

    def accumulate(group, blocks):
        lhs, rhs = [], []
        for q in range(GROUP):
            pair = group * GROUP + q
            row = (pair + steps - blocks) * blk
            lhs.append(coda_t[pl.ds(pl.multiple_of(row, blk), blocks * blk), :])
            first = (2 * pair + win * share) * blk
            rhs.append(
                jnp.concatenate(
                    [coda[pl.ds(pl.multiple_of(first + b * blk, blk), 2 * blk), :] for b in range(2)], axis=1
                )
            )
        value = jnp.dot(
            jnp.concatenate(lhs, axis=1), jnp.concatenate(rhs, axis=0), preferred_element_type=f32
        )
        acc[(steps - blocks) * blk :, :] += value

    peeled = steps // GROUP - 1
    for group in range(peeled):
        accumulate(group, (group + 1) * GROUP)
    groups = pairs // GROUP - win * (share // (2 * GROUP))

    def whole(group, _):
        accumulate(group, steps)
        return 0

    lax.fori_loop(peeled, groups, whole, 0)
    for i in range(steps):
        for b in range(2):
            lag = 2 * (steps - 1 - i) + b
            rows[pl.ds(lag, blk, stride=share + ROW_PAD), :] = (
                acc[i * blk : (i + 1) * blk, b * blk : (b + 1) * blk] * scale_three
            )
    out_ref[...] = rows[...].reshape(blk, share + ROW_PAD, blk)[:, :share].astype(bf16)


def pair_kernel(windows, win_ref, *refs):
    own_ref, partner_ref = refs[:windows], refs[windows : 2 * windows]
    out_ref, shifted, partner_t, rows = refs[2 * windows :]
    rounds, blk, length = partner_ref[0].shape
    share = out_ref.shape[2]
    scale_two = 1.0 / math.sqrt(windows * length)
    win = win_ref[0]
    for w in range(windows):
        for r in range(rounds):
            partner_t[w, :length, r * blk : (r + 1) * blk] = partner_ref[w][r].T
        partner_t[w, length:, :] = jnp.zeros((partner_t.shape[1] - length, rounds * blk), bf16)
        samples = own_ref[w][...].astype(f32)
        for b in range(STEP):
            shifted[b * blk : (b + 1) * blk, w * length : (w + 1) * length] = shift_right(samples, b)

    half = STEP // 2

    def pair(step, _):
        a = step // 2
        b_half = step % 2
        first = pl.multiple_of(win * share + a * STEP, STEP)
        weights = jnp.concatenate([partner_t[w, pl.ds(first, length), :] for w in range(windows)], axis=0)
        row = pl.multiple_of(b_half * half * blk, blk)
        result = jnp.dot(shifted[pl.ds(row, half * blk), :], weights, preferred_element_type=f32)
        for b in range(half):
            lag = a * STEP + b_half * half + b
            for r in range(rounds):
                rows[r, pl.ds(lag, blk, stride=share + ROW_PAD), :] = (
                    result[b * blk : (b + 1) * blk, r * blk : (r + 1) * blk] * scale_two
                )
        return 0

    lax.fori_loop(0, 2 * (share // STEP), pair, 0)
    for r in range(rounds):
        out_ref[r] = rows[r].reshape(blk, share + ROW_PAD, blk)[:, :share].astype(bf16)


def coda_coherence(win, aux, own, start, end, share):
    windows = len(own)
    blk, length = own[0].shape
    used = length - CODA_LO
    steps = share // 2
    return pl.pallas_call(
        functools.partial(coda_kernel, windows),
        out_shape=jax.ShapeDtypeStruct((blk, share, blk), bf16),
        in_specs=[SMEM_SPEC] + [VMEM_SPEC] * (2 + 2 * windows),
        out_specs=VMEM_SPEC,
        scratch_shapes=[
            pltpu.VMEM((STEP * blk, windows * used), bf16),
            pltpu.VMEM((windows, length + CODA, blk), bf16),
            pltpu.VMEM(((CODA + 1) * blk, blk), bf16),
            pltpu.VMEM(((CODA // 2 + steps - 1) * blk, 2 * blk), bf16),
            pltpu.VMEM((steps * blk, 2 * blk), f32),
            pltpu.VMEM(((share + ROW_PAD) * blk, blk), f32),
        ],
        compiler_params=pltpu.CompilerParams(vmem_limit_bytes=VMEM_LIMIT),
        name="coda_coherence",
    )(win, start, end, *aux, *own)


def pair_coherence(win, own, partner, share):
    windows = len(own)
    rounds, blk, length = partner[0].shape
    return pl.pallas_call(
        functools.partial(pair_kernel, windows),
        out_shape=jax.ShapeDtypeStruct((rounds, blk, share, blk), bf16),
        in_specs=[SMEM_SPEC] + [VMEM_SPEC] * (2 * windows),
        out_specs=VMEM_SPEC,
        scratch_shapes=[
            pltpu.VMEM((STEP * blk, windows * length), bf16),
            pltpu.VMEM((windows, length + LAGS, rounds * blk), bf16),
            pltpu.VMEM((rounds, blk * (share + ROW_PAD), blk), f32),
        ],
        compiler_params=pltpu.CompilerParams(vmem_limit_bytes=VMEM_LIMIT),
        name="pair_coherence",
    )(win, *own, *partner)


def per_device(traces, pairing, aux_owners, coda_start, coda_end):
    win_size = lax.axis_size("win")
    chan_size = lax.axis_size("chan")
    win_index = lax.axis_index("win")
    chan_index = lax.axis_index("chan")
    blk = traces.shape[1]
    rounds = pairing.shape[0]
    white = whiten(traces)

    def exchange(block, k):
        return lax.ppermute(block, "win", [(i, i ^ k) for i in range(win_size)])

    own_all = [white] + [exchange(white, k) for k in range(1, win_size)]
    column = [white] + [
        lax.ppermute(white, "chan", [(i, (i + 2 * k) % chan_size) for i in range(chan_size)])
        for k in range(1, chan_size // 2)
    ]

    own_all, column = lax.optimization_barrier((own_all, column))

    def look_up(block):
        steps = jnp.mod(chan_index - block, chan_size) // 2
        found = column[0]
        for k in range(1, chan_size // 2):
            found = jnp.where(steps == k, column[k], found)
        return found

    def wanted(chan):
        return [aux_owners[0]] + [pairing[r, chan] for r in range(rounds)]

    asked = jnp.stack([look_up(block) for block in wanted(chan_index ^ 1)])
    answered = lax.ppermute(asked, "chan", [(i, i ^ 1) for i in range(chan_size)])
    blocks = [
        jnp.where((block - chan_index) % 2 == 0, look_up(block), answered[n])
        for n, block in enumerate(wanted(chan_index))
    ]
    aux = blocks[0]
    partners = jnp.stack(blocks[1:])
    aux_all = [aux] + [exchange(aux, k) for k in range(1, win_size)]
    partners, *aux_all = lax.optimization_barrier((partners, *aux_all))
    partner_all = [partners] + [exchange(partners, k) for k in range(1, win_size)]
    win = win_index.reshape(1).astype(jnp.int32)
    start = jnp.broadcast_to(coda_start[0][:, None], (blk, blk))
    end = jnp.broadcast_to(coda_end[0][:, None], (blk, blk))
    three = coda_coherence(win, aux_all, own_all, start, end, LAGS3 // win_size)
    pair = pair_coherence(win, own_all, partner_all, LAGS // win_size)
    return (pair, three)


def solution(mesh):
    in_specs = (P("win", "chan", None), P(), P(), P(), P())
    out_specs = (P(None, "chan", "win", None), P("chan", "win", None))
    return jax.shard_map(per_device, mesh=mesh, in_specs=in_specs, out_specs=out_specs, check_vma=False)
```

```python
import functools
import math

import jax
import jax.numpy as jnp
from jax import lax
from jax.experimental import pallas as pl
from jax.experimental.pallas import tpu as pltpu
from jax.sharding import PartitionSpec as P

LAGS = 256
CODA = 128
CODA_LO = 128
LAGS3 = 128
EPS = 1e-05
STEP = 16
GROUP = 4

SMEM_SPEC = pl.BlockSpec(memory_space=pltpu.SMEM)
VMEM_SPEC = pl.BlockSpec(memory_space=pltpu.VMEM)
ROW_PAD = 8

f32 = jnp.float32
bf16 = jnp.bfloat16


def whiten_kernel(traces_ref, out_ref):
    samples = traces_ref[0].astype(f32)
    energy_mean = jnp.mean(samples * samples, axis=-1, keepdims=True)
    out_ref[...] = (samples * lax.rsqrt(energy_mean + EPS)).astype(bf16)


def whiten(traces):
    return pl.pallas_call(
        whiten_kernel,
        out_shape=jax.ShapeDtypeStruct(traces.shape[1:], bf16),
        in_specs=[VMEM_SPEC],
        out_specs=VMEM_SPEC,
        name="whiten",
    )(traces)


def shift_right(block, count):
    if count == 0:
        return block.astype(bf16)
    moved = pltpu.roll(block, count, 1)
    lane = lax.broadcasted_iota(jnp.int32, block.shape, 1)
    return jnp.where(lane < count, 0.0, moved).astype(bf16)


def pick_kernel(count, which_ref, *refs):
    column, out_refs = refs[:count], refs[count:]
    slots = [out_refs[0], out_refs[1]]
    for out_ref in out_refs[2:]:
        slots += [out_ref.at[r] for r in range(out_ref.shape[0])]
    for n, slot in enumerate(slots):
        for k in range(count):

            @pl.when(which_ref[n] == k)
            def _():
                slot[...] = column[k][...]


def pick(which, column, rounds):
    block = column[0].shape
    shapes = [block, block, (rounds,) + block, (rounds,) + block]
    return pl.pallas_call(
        functools.partial(pick_kernel, len(column)),
        out_shape=[jax.ShapeDtypeStruct(shape, bf16) for shape in shapes],
        in_specs=[SMEM_SPEC] + [VMEM_SPEC] * len(column),
        out_specs=[VMEM_SPEC] * 4,
        compiler_params=pltpu.CompilerParams(vmem_limit_bytes=2 << 20),
        name="pick",
    )(which, *column)


def merge_kernel(crossed_ref, held_ref, got_ref, out_ref):
    for r in range(held_ref.shape[0]):

        @pl.when(crossed_ref[r] == 0)
        def _():
            out_ref[r] = held_ref[r]

        @pl.when(crossed_ref[r] != 0)
        def _():
            out_ref[r] = got_ref[r]


def merge(crossed, held, got):
    return pl.pallas_call(
        merge_kernel,
        out_shape=jax.ShapeDtypeStruct(held.shape, bf16),
        in_specs=[SMEM_SPEC, VMEM_SPEC, VMEM_SPEC],
        out_specs=VMEM_SPEC,
        compiler_params=pltpu.CompilerParams(vmem_limit_bytes=2 << 20),
        name="merge",
    )(crossed, held, got)


def shift_kernel(block_ref, out_ref):
    blk, length = block_ref.shape
    lane = lax.broadcasted_iota(jnp.int32, (STEP, length), 1)
    row = lax.broadcasted_iota(jnp.int32, (STEP, length), 0)
    for i in range(blk):
        samples = jnp.broadcast_to(block_ref[i : i + 1, :].astype(f32), (STEP, length))
        moved = pltpu.roll(samples, 0, 1, stride=1, stride_axis=0)
        out_ref[i * STEP : (i + 1) * STEP, :] = jnp.where(lane < row, 0.0, moved).astype(bf16)


def shifted_copies(block):
    blk, length = block.shape
    return pl.pallas_call(
        shift_kernel,
        out_shape=jax.ShapeDtypeStruct((blk * STEP, length), bf16),
        in_specs=[VMEM_SPEC],
        out_specs=VMEM_SPEC,
        compiler_params=pltpu.CompilerParams(vmem_limit_bytes=4 << 20),
        name="shifted_copies",
    )(block)


def part_first_kernel(aux_ref, own_ref, out_ref, shifted, own_t):
    blk, length = own_ref.shape
    used = length - CODA_LO
    step = pl.program_id(0)

    @pl.when(step == 0)
    def _():
        own_t[:length, :] = own_ref[...].T
        own_t[length:, :] = jnp.zeros((own_t.shape[0] - length, blk), bf16)
        samples = aux_ref[...][:, :used].astype(f32)
        for b in range(STEP):
            shifted[b * blk : (b + 1) * blk, :] = shift_right(samples, b)

    halves = [
        own_t[pl.ds(pl.multiple_of(CODA_LO + (2 * step + a) * STEP, STEP), used), :] for a in range(2)
    ]
    out_ref[0] = jnp.dot(shifted[...], jnp.concatenate(halves, axis=1), preferred_element_type=f32)


def part_first(aux, own):
    blk, length = own.shape
    used = length - CODA_LO
    steps = CODA // (2 * STEP)
    return pl.pallas_call(
        part_first_kernel,
        out_shape=jax.ShapeDtypeStruct((steps, STEP * blk, 2 * blk), f32),
        grid=(steps,),
        in_specs=[VMEM_SPEC] * 2,
        out_specs=pl.BlockSpec((1, STEP * blk, 2 * blk), lambda step: (step, 0, 0)),
        scratch_shapes=[pltpu.VMEM((STEP * blk, used), bf16), pltpu.VMEM((length + CODA, blk), bf16)],
        compiler_params=pltpu.CompilerParams(vmem_limit_bytes=16 << 20),
        cost_estimate=pl.CostEstimate(
            flops=2 * CODA * blk * blk * used, transcendentals=0, bytes_accessed=4 * CODA * blk * blk
        ),
        name="part_first",
    )(aux, own)


def coda_kernel(windows, win_ref, start_ref, end_ref, first, *refs):
    aux_ref, own_ref = refs[:windows], refs[windows : 2 * windows]
    out_ref, shifted, own_t, limits, coda, coda_t, acc, rows = refs[2 * windows :]
    blk, length = own_ref[0].shape
    used = length - CODA_LO
    share = out_ref.shape[1]
    steps = share // 2
    pairs = CODA // 2
    scale_two = 1.0 / math.sqrt((windows + 1) * length)
    scale_three = 1.0 / math.sqrt(blk * CODA)
    win = win_ref[0]

    limits[0] = jnp.broadcast_to(start_ref[...], (blk, blk)).T
    limits[1] = jnp.broadcast_to(end_ref[...], (blk, blk)).T
    for w in range(windows):
        own_t[w, :length, :] = own_ref[w][...].T
        own_t[w, length:, :] = jnp.zeros((own_t.shape[1] - length, blk), bf16)
        samples = aux_ref[w][:, :used].astype(f32)
        for b in range(STEP):
            shifted[b * blk : (b + 1) * blk, w * used : (w + 1) * used] = shift_right(samples, b)
    coda[CODA * blk :, :] = jnp.zeros((coda.shape[0] - CODA * blk, blk), bf16)
    coda_t[: (steps - 1) * blk, :] = jnp.zeros(((steps - 1) * blk, 2 * blk), bf16)
    acc[...] = jnp.zeros(acc.shape, f32)

    half = STEP // 2

    def part(step, _):
        a_pair = step // 2
        b_half = step % 2
        pieces = []
        for w in range(windows):
            halves = [
                own_t[w, pl.ds(pl.multiple_of(CODA_LO + (2 * a_pair + a) * STEP, STEP), used), :]
                for a in range(2)
            ]
            pieces.append(jnp.concatenate(halves, axis=1))
        weights = jnp.concatenate(pieces, axis=0)
        row = pl.multiple_of(b_half * half * blk, blk)
        result = jnp.dot(shifted[pl.ds(row, half * blk), :], weights, preferred_element_type=f32)
        for b in range(half):
            for a in range(2):
                lag = (2 * a_pair + a) * STEP + b_half * half + b
                earlier = first[a_pair, pl.ds(row + b * blk, blk), a * blk : (a + 1) * blk]
                tile = (result[b * blk : (b + 1) * blk, a * blk : (a + 1) * blk] + earlier) * scale_two
                live = (lag >= limits[0]) & (lag < limits[1])
                tile = jnp.where(live, tile, 0.0)
                coda[pl.ds(pl.multiple_of(lag * blk, blk), blk), :] = tile.astype(bf16)
                place = pl.multiple_of((lag // 2 + steps - 1) * blk, blk)
                coda_t[pl.ds(place, blk), (b % 2) * blk : (b % 2 + 1) * blk] = tile.T.astype(bf16)
        return 0

    lax.fori_loop(0, CODA // STEP, part, 0)

    def accumulate(group, blocks):
        lhs, rhs = [], []
        for q in range(GROUP):
            pair = group * GROUP + q
            row = (pair + steps - blocks) * blk
            lhs.append(coda_t[pl.ds(pl.multiple_of(row, blk), blocks * blk), :])
            top = (2 * pair + win * share) * blk
            rhs.append(
                jnp.concatenate(
                    [coda[pl.ds(pl.multiple_of(top + b * blk, blk), 2 * blk), :] for b in range(2)], axis=1
                )
            )
        value = jnp.dot(
            jnp.concatenate(lhs, axis=1), jnp.concatenate(rhs, axis=0), preferred_element_type=f32
        )
        acc[(steps - blocks) * blk :, :] += value

    peeled = steps // GROUP - 1
    for group in range(peeled):
        accumulate(group, (group + 1) * GROUP)
    groups = pairs // GROUP - win * (share // (2 * GROUP))

    def whole(group, _):
        accumulate(group, steps)
        return 0

    lax.fori_loop(peeled, groups, whole, 0)
    for i in range(steps):
        for b in range(2):
            lag = 2 * (steps - 1 - i) + b
            rows[pl.ds(lag, blk, stride=share + ROW_PAD), :] = (
                acc[i * blk : (i + 1) * blk, b * blk : (b + 1) * blk] * scale_three
            )
    out_ref[...] = rows[...].reshape(blk, share + ROW_PAD, blk)[:, :share].astype(bf16)


def coda_limit(windows, blk, used):
    return (21 << 20) + 2 * STEP * blk * windows * used


def coda_coherence(win, start, end, first, aux, own, share):
    windows = len(own)
    blk, length = own[0].shape
    used = length - CODA_LO
    steps = share // 2
    return pl.pallas_call(
        functools.partial(coda_kernel, windows),
        out_shape=jax.ShapeDtypeStruct((blk, share, blk), bf16),
        in_specs=[SMEM_SPEC] + [VMEM_SPEC] * (3 + 2 * windows),
        out_specs=VMEM_SPEC,
        scratch_shapes=[
            pltpu.VMEM((STEP * blk, windows * used), bf16),
            pltpu.VMEM((windows, length + CODA, blk), bf16),
            pltpu.VMEM((2, blk, blk), jnp.int32),
            pltpu.VMEM(((CODA + 1) * blk, blk), bf16),
            pltpu.VMEM(((CODA // 2 + steps - 1) * blk, 2 * blk), bf16),
            pltpu.VMEM((steps * blk, 2 * blk), f32),
            pltpu.VMEM(((share + ROW_PAD) * blk, blk), f32),
        ],
        compiler_params=pltpu.CompilerParams(vmem_limit_bytes=coda_limit(windows, blk, used)),
        name="coda_coherence",
    )(win, start, end, first, *aux, *own)


def transpose_partners(partner_ref, partner_t):
    rounds, blk, length = partner_ref.shape
    for r in range(rounds):
        partner_t[:length, r * blk : (r + 1) * blk] = partner_ref[r].T
    partner_t[length:, :] = jnp.zeros((partner_t.shape[0] - length, rounds * blk), bf16)


def pair_first_kernel(win_ref, shifted_ref, partner_ref, out_ref, partner_t):
    length = partner_ref.shape[2]
    steps = pl.num_programs(0)
    step = pl.program_id(0)

    @pl.when(step == 0)
    def _():
        transpose_partners(partner_ref, partner_t)

    top = pl.multiple_of((win_ref[0] * steps + step) * STEP, STEP)
    out_ref[0] = jnp.dot(shifted_ref[...], partner_t[pl.ds(top, length), :], preferred_element_type=f32)


def pair_first(win, shifted, partner, share):
    rounds, blk, length = partner.shape
    steps = share // STEP
    return pl.pallas_call(
        pair_first_kernel,
        out_shape=jax.ShapeDtypeStruct((steps, blk * STEP, rounds * blk), f32),
        grid=(steps,),
        in_specs=[SMEM_SPEC, VMEM_SPEC, VMEM_SPEC],
        out_specs=pl.BlockSpec((1, blk * STEP, rounds * blk), lambda step: (step, 0, 0)),
        scratch_shapes=[pltpu.VMEM((length + LAGS, rounds * blk), bf16)],
        compiler_params=pltpu.CompilerParams(vmem_limit_bytes=12 << 20),
        cost_estimate=pl.CostEstimate(
            flops=2 * share * rounds * blk * blk * length,
            transcendentals=0,
            bytes_accessed=4 * share * rounds * blk * blk,
        ),
        name="pair_first",
    )(win, shifted, partner)


def pair_kernel(windows, win_ref, first_ref, *refs):
    shifted, partner_ref = refs[:windows], refs[windows : 2 * windows]
    out_ref, partner_t = refs[2 * windows :]
    rounds, blk, length = partner_ref[0].shape
    scale_two = 1.0 / math.sqrt((windows + 1) * length)
    steps = pl.num_programs(0)
    step = pl.program_id(0)

    @pl.when(step == 0)
    def _():
        for w in range(windows):
            transpose_partners(partner_ref[w], partner_t.at[w])

    top = pl.multiple_of((win_ref[0] * steps + step) * STEP, STEP)
    weights = jnp.concatenate([partner_t[w, pl.ds(top, length), :] for w in range(windows)], axis=0)
    half = blk // 2
    for part in range(2):
        rows = slice(part * half * STEP, (part + 1) * half * STEP)
        samples = jnp.concatenate([shifted[w][rows, :] for w in range(windows)], axis=1)
        result = jnp.dot(samples, weights, preferred_element_type=f32)
        result = ((result + first_ref[0, rows, :]) * scale_two).astype(bf16)
        for r in range(rounds):
            out_ref[r, part * half : (part + 1) * half] = result[:, r * blk : (r + 1) * blk].reshape(
                half, STEP, blk
            )


def pair_coherence(win, first, shifted, partner, share):
    windows = len(shifted)
    rounds, blk, length = partner[0].shape
    steps = share // STEP
    return pl.pallas_call(
        functools.partial(pair_kernel, windows),
        out_shape=jax.ShapeDtypeStruct((rounds, blk, share, blk), bf16),
        grid=(steps,),
        in_specs=[SMEM_SPEC, pl.BlockSpec((1,) + first.shape[1:], lambda step: (step, 0, 0))]
        + [VMEM_SPEC] * (2 * windows),
        out_specs=pl.BlockSpec((rounds, blk, STEP, blk), lambda step: (0, 0, step, 0)),
        scratch_shapes=[pltpu.VMEM((windows, length + LAGS, rounds * blk), bf16)],
        compiler_params=pltpu.CompilerParams(vmem_limit_bytes=20 << 20),
        name="pair_coherence",
    )(win, first, *shifted, *partner)


def per_device(traces, pairing, aux_owners, coda_start, coda_end):
    win_size = lax.axis_size("win")
    chan_size = lax.axis_size("chan")
    win_index = lax.axis_index("win")
    chan_index = lax.axis_index("chan")
    blk = traces.shape[1]
    rounds = pairing.shape[0]
    wanted = jnp.concatenate(
        [
            aux_owners,
            aux_owners,
            lax.dynamic_index_in_dim(pairing, chan_index ^ 1, 1, keepdims=False),
            lax.dynamic_index_in_dim(pairing, chan_index, 1, keepdims=False),
        ]
    )
    which = jnp.mod(chan_index - wanted, chan_size) // 2
    crossed = jnp.mod(chan_index - wanted, 2)
    aux_crossed, crossed = crossed[:1], crossed[2 + rounds :]
    win = win_index.reshape(1).astype(jnp.int32)
    traces, which, aux_crossed, crossed, win = lax.optimization_barrier(
        (traces, which, aux_crossed, crossed, win)
    )
    white = whiten(traces)

    def exchange(block, k):
        return lax.ppermute(block, "win", [(i, i ^ k) for i in range(win_size)])

    def cross(block):
        return lax.ppermute(block, "chan", [(i, i ^ 1) for i in range(chan_size)])

    column = [white] + [
        lax.ppermute(white, "chan", [(i, (i + 2 * k) % chan_size) for i in range(chan_size)])
        for k in range(1, chan_size // 2)
    ]
    own_all = [white] + [exchange(white, k) for k in range(1, win_size)]
    copies = [shifted_copies(block) for block in own_all]
    own_all, first_copies, column = lax.optimization_barrier((own_all, copies[0], column))
    aux_sent, aux_held, sent, held = pick(which, column, rounds)
    aux = merge(aux_crossed, aux_held[None], cross(aux_sent)[None])[0]
    partners = merge(crossed, held, cross(sent))
    aux_rest = [exchange(aux, k) for k in range(1, win_size)]
    pair_begun = pair_first(win, first_copies, partners, LAGS // win_size)
    part_begun = part_first(aux, own_all[0])
    partners, aux_rest, pair_begun, part_begun, copies = lax.optimization_barrier(
        (partners, aux_rest, pair_begun, part_begun, copies[1:])
    )
    partner_rest = [exchange(partners, k) for k in range(1, win_size)]
    three = coda_coherence(
        win, coda_start, coda_end, part_begun, aux_rest, own_all[1:], LAGS3 // win_size
    )
    pair = pair_coherence(win, pair_begun, copies, partner_rest, LAGS // win_size)
    return (pair, three)


def solution(mesh):
    in_specs = (P("win", "chan", None), P(), P(), P(), P())
    out_specs = (P(None, "chan", "win", None), P("chan", "win", None))
    return jax.shard_map(per_device, mesh=mesh, in_specs=in_specs, out_specs=out_specs, check_vma=False)
```

```python
import functools
import math

import jax
import jax.numpy as jnp
from jax import lax
from jax.experimental import pallas as pl
from jax.experimental.pallas import tpu as pltpu
from jax.sharding import PartitionSpec as P

LAGS = 256
CODA = 128
CODA_LO = 128
LAGS3 = 128
EPS = 1e-05
STEP = 16
GROUP = 4

SMEM_SPEC = pl.BlockSpec(memory_space=pltpu.SMEM)
VMEM_SPEC = pl.BlockSpec(memory_space=pltpu.VMEM)
ROW_PAD = 8

f32 = jnp.float32
bf16 = jnp.bfloat16


def white_block(traces):
    samples = traces.astype(f32)
    energy_mean = jnp.mean(samples * samples, axis=-1, keepdims=True)
    return (samples * lax.rsqrt(energy_mean + EPS)).astype(bf16)


def shift_right(block, count):
    if count == 0:
        return block.astype(bf16)
    moved = pltpu.roll(block, count, 1)
    lane = lax.broadcasted_iota(jnp.int32, block.shape, 1)
    return jnp.where(lane < count, 0.0, moved).astype(bf16)


def pick_kernel(rounds, owners_ref, pairing_ref, *refs):
    column, out_refs = refs[:-4], refs[-4:]
    count = len(column)
    chan = lax.axis_index("chan")
    other = chan + 1 - 2 * (chan % 2)
    aux = owners_ref[0]
    slots = [(out_refs[0], aux), (out_refs[1], aux)]
    slots += [(out_refs[2].at[r], pairing_ref[r, other]) for r in range(rounds)]
    slots += [(out_refs[3].at[r], pairing_ref[r, chan]) for r in range(rounds)]
    for slot, block in slots:
        distance = (chan - block + 2 * count) % (2 * count) // 2
        for k in range(count):

            @pl.when(distance == k)
            def _():
                slot[...] = column[k][...]


def pick(owners, pairing, column):
    block = column[0].shape
    rounds = pairing.shape[0]
    shapes = [block, block, (rounds,) + block, (rounds,) + block]
    return pl.pallas_call(
        functools.partial(pick_kernel, rounds),
        out_shape=[jax.ShapeDtypeStruct(shape, bf16) for shape in shapes],
        in_specs=[SMEM_SPEC] * 2 + [VMEM_SPEC] * len(column),
        out_specs=[VMEM_SPEC] * 4,
        compiler_params=pltpu.CompilerParams(vmem_limit_bytes=2 << 20),
        name="pick",
    )(owners, pairing, *column)


def merge(blocks_of, scalars, held, got):
    def kernel(scalars_ref, held_ref, got_ref, out_ref):
        chan = lax.axis_index("chan")
        for r, block in enumerate(blocks_of(scalars_ref, chan)):
            same = (chan + block) % 2 == 0
            here, sent, out = (ref if len(ref.shape) == 2 else ref.at[r] for ref in (held_ref, got_ref, out_ref))

            @pl.when(same)
            def _():
                out[...] = white_block(here[...])

            @pl.when(jnp.logical_not(same))
            def _():
                out[...] = white_block(sent[...])

    return pl.pallas_call(
        kernel,
        out_shape=jax.ShapeDtypeStruct(held.shape, bf16),
        in_specs=[SMEM_SPEC, VMEM_SPEC, VMEM_SPEC],
        out_specs=VMEM_SPEC,
        compiler_params=pltpu.CompilerParams(vmem_limit_bytes=4 << 20),
        name="merge",
    )(scalars, held, got)


def shift_kernel(block_ref, out_ref, white_ref, *raw_ref):
    for ref in raw_ref:
        ref[...] = block_ref[...]
    white_ref[...] = white_block(block_ref[...])
    blk, length = block_ref.shape
    lane = lax.broadcasted_iota(jnp.int32, (STEP, length), 1)
    row = lax.broadcasted_iota(jnp.int32, (STEP, length), 0)
    for i in range(blk):
        samples = jnp.broadcast_to(white_ref[i : i + 1, :].astype(f32), (STEP, length))
        moved = pltpu.roll(samples, 0, 1, stride=1, stride_axis=0)
        out_ref[i * STEP : (i + 1) * STEP, :] = jnp.where(lane < row, 0.0, moved).astype(bf16)


def shifted_copies(block, raw=False):
    blk, length = block.shape
    return pl.pallas_call(
        shift_kernel,
        out_shape=[
            jax.ShapeDtypeStruct((blk * STEP, length), bf16),
            jax.ShapeDtypeStruct((blk, length), bf16),
        ]
        + [jax.ShapeDtypeStruct((blk, length), bf16)] * raw,
        in_specs=[VMEM_SPEC],
        out_specs=[VMEM_SPEC] * (2 + raw),
        compiler_params=pltpu.CompilerParams(vmem_limit_bytes=4 << 20),
        name="shifted_copies",
    )(block)


def part_first_kernel(aux_ref, own_ref, out_ref, shifted, own_t):
    blk, length = own_ref.shape
    used = length - CODA_LO
    step = pl.program_id(0)

    @pl.when(step == 0)
    def _():
        own_t[:length, :] = own_ref[...].T
        own_t[length:, :] = jnp.zeros((own_t.shape[0] - length, blk), bf16)
        samples = aux_ref[...][:, :used].astype(f32)
        for b in range(STEP):
            shifted[b * blk : (b + 1) * blk, :] = shift_right(samples, b)

    halves = [
        own_t[pl.ds(pl.multiple_of(CODA_LO + (2 * step + a) * STEP, STEP), used), :] for a in range(2)
    ]
    out_ref[0] = jnp.dot(shifted[...], jnp.concatenate(halves, axis=1), preferred_element_type=f32)


def part_first(aux, own):
    blk, length = own.shape
    used = length - CODA_LO
    steps = CODA // (2 * STEP)
    return pl.pallas_call(
        part_first_kernel,
        out_shape=jax.ShapeDtypeStruct((steps, STEP * blk, 2 * blk), f32),
        grid=(steps,),
        in_specs=[VMEM_SPEC] * 2,
        out_specs=pl.BlockSpec((1, STEP * blk, 2 * blk), lambda step: (step, 0, 0)),
        scratch_shapes=[pltpu.VMEM((STEP * blk, used), bf16), pltpu.VMEM((length + CODA, blk), bf16)],
        compiler_params=pltpu.CompilerParams(vmem_limit_bytes=16 << 20),
        cost_estimate=pl.CostEstimate(
            flops=2 * CODA * blk * blk * used, transcendentals=0, bytes_accessed=4 * CODA * blk * blk
        ),
        name="part_first",
    )(aux, own)


def coda_kernel(windows, start_ref, end_ref, first, *refs):
    aux_ref, own_ref = refs[:windows], refs[windows : 2 * windows]
    out_ref, shifted, own_t, limits, coda, coda_t, acc, rows = refs[2 * windows :]
    blk, length = own_ref[0].shape
    used = length - CODA_LO
    share = out_ref.shape[1]
    steps = share // 2
    pairs = CODA // 2
    scale_two = 1.0 / math.sqrt((windows + 1) * length)
    scale_three = 1.0 / math.sqrt(blk * CODA)
    win = lax.axis_index("win")

    limits[0] = jnp.broadcast_to(start_ref[...], (blk, blk)).T
    limits[1] = jnp.broadcast_to(end_ref[...], (blk, blk)).T
    for w in range(windows):
        own_t[w, :length, :] = own_ref[w][...].T
        own_t[w, length:, :] = jnp.zeros((own_t.shape[1] - length, blk), bf16)
        samples = aux_ref[w][:, :used].astype(f32)
        for b in range(STEP):
            shifted[b * blk : (b + 1) * blk, w * used : (w + 1) * used] = shift_right(samples, b)
    coda[CODA * blk :, :] = jnp.zeros((coda.shape[0] - CODA * blk, blk), bf16)
    coda_t[: (steps - 1) * blk, :] = jnp.zeros(((steps - 1) * blk, 2 * blk), bf16)
    acc[...] = jnp.zeros(acc.shape, f32)

    chunk = STEP // 2

    def part(a_pair, limit):
        pieces = []
        for w in range(windows):
            halves = [
                own_t[w, pl.ds(pl.multiple_of(CODA_LO + (2 * a_pair + a) * STEP, STEP), used), :]
                for a in range(2)
            ]
            pieces.append(jnp.concatenate(halves, axis=1))
        weights = jnp.concatenate(pieces, axis=0)
        for b_first in range(0, STEP, chunk):
            rows_here = slice(b_first * blk, (b_first + chunk) * blk)
            result = jnp.dot(shifted[rows_here, :], weights, preferred_element_type=f32)
            result = (result + first[a_pair, rows_here, :]) * scale_two
            for b in range(chunk):
                for a in range(2):
                    lag = (2 * a_pair + a) * STEP + b_first + b
                    tile = result[b * blk : (b + 1) * blk, a * blk : (a + 1) * blk]
                    if limit == 0:
                        tile = jnp.where(lag >= limits[0], tile, 0.0)
                    if limit == 1:
                        tile = jnp.where(lag < limits[1], tile, 0.0)
                    tile = tile.astype(bf16)
                    coda[pl.ds(pl.multiple_of(lag * blk, blk), blk), :] = tile
                    place = pl.multiple_of((lag // 2 + steps - 1) * blk, blk)
                    coda_t[pl.ds(place, blk), (b % 2) * blk : (b % 2 + 1) * blk] = tile.T

    def run(first_step, last_step, limit):
        def body(step, _):
            part(step, limit)
            return 0

        lax.fori_loop(first_step, last_step, body, 0)

    count = CODA // (2 * STEP)
    run(0, count // 4, 0)
    run(count // 4, 3 * count // 4, None)
    run(3 * count // 4, count, 1)

    def accumulate(group, blocks):
        lhs, rhs = [], []
        for q in range(GROUP):
            pair = group * GROUP + q
            row = (pair + steps - blocks) * blk
            lhs.append(coda_t[pl.ds(pl.multiple_of(row, blk), blocks * blk), :])
            top = (2 * pair + win * share) * blk
            rhs.append(
                jnp.concatenate(
                    [coda[pl.ds(pl.multiple_of(top + b * blk, blk), 2 * blk), :] for b in range(2)], axis=1
                )
            )
        value = jnp.dot(
            jnp.concatenate(lhs, axis=1), jnp.concatenate(rhs, axis=0), preferred_element_type=f32
        )
        acc[(steps - blocks) * blk :, :] += value

    peeled = steps // GROUP - 1
    for group in range(peeled):
        accumulate(group, (group + 1) * GROUP)
    groups = pairs // GROUP - win * (share // (2 * GROUP))

    def whole(group, _):
        accumulate(group, steps)
        return 0

    lax.fori_loop(peeled, groups, whole, 0)
    for i in range(steps):
        for b in range(2):
            lag = 2 * (steps - 1 - i) + b
            rows[pl.ds(lag, blk, stride=share + ROW_PAD), :] = (
                acc[i * blk : (i + 1) * blk, b * blk : (b + 1) * blk] * scale_three
            )
    out_ref[...] = rows[...].reshape(blk, share + ROW_PAD, blk)[:, :share].astype(bf16)


def coda_limit(windows, blk, used):
    return (21 << 20) + 2 * STEP * blk * windows * used


def coda_coherence(start, end, first, aux, own, share):
    windows = len(own)
    blk, length = own[0].shape
    used = length - CODA_LO
    steps = share // 2
    return pl.pallas_call(
        functools.partial(coda_kernel, windows),
        out_shape=jax.ShapeDtypeStruct((blk, share, blk), bf16),
        in_specs=[VMEM_SPEC] * (3 + 2 * windows),
        out_specs=VMEM_SPEC,
        scratch_shapes=[
            pltpu.VMEM((STEP * blk, windows * used), bf16),
            pltpu.VMEM((windows, length + CODA, blk), bf16),
            pltpu.VMEM((2, blk, blk), jnp.int32),
            pltpu.VMEM(((CODA + 1) * blk, blk), bf16),
            pltpu.VMEM(((CODA // 2 + steps - 1) * blk, 2 * blk), bf16),
            pltpu.VMEM((steps * blk, 2 * blk), f32),
            pltpu.VMEM(((share + ROW_PAD) * blk, blk), f32),
        ],
        compiler_params=pltpu.CompilerParams(vmem_limit_bytes=coda_limit(windows, blk, used)),
        name="coda_coherence",
    )(start, end, first, *aux, *own)


def transpose_partners(partner_ref, partner_t):
    rounds, blk, length = partner_ref.shape
    for r in range(rounds):
        partner_t[:length, r * blk : (r + 1) * blk] = partner_ref[r].T
    partner_t[length:, :] = jnp.zeros((partner_t.shape[0] - length, rounds * blk), bf16)


def pair_first_kernel(shifted_ref, partner_ref, out_ref, partner_t):
    length = partner_ref.shape[2]
    steps = pl.num_programs(0)
    step = pl.program_id(0)

    @pl.when(step == 0)
    def _():
        transpose_partners(partner_ref, partner_t)

    top = pl.multiple_of((lax.axis_index("win") * steps + step) * STEP, STEP)
    out_ref[0] = jnp.dot(shifted_ref[...], partner_t[pl.ds(top, length), :], preferred_element_type=f32)


def pair_first(shifted, partner, share):
    rounds, blk, length = partner.shape
    steps = share // STEP
    return pl.pallas_call(
        pair_first_kernel,
        out_shape=jax.ShapeDtypeStruct((steps, blk * STEP, rounds * blk), f32),
        grid=(steps,),
        in_specs=[VMEM_SPEC, VMEM_SPEC],
        out_specs=pl.BlockSpec((1, blk * STEP, rounds * blk), lambda step: (step, 0, 0)),
        scratch_shapes=[pltpu.VMEM((length + LAGS, rounds * blk), bf16)],
        compiler_params=pltpu.CompilerParams(vmem_limit_bytes=12 << 20),
        cost_estimate=pl.CostEstimate(
            flops=2 * share * rounds * blk * blk * length,
            transcendentals=0,
            bytes_accessed=4 * share * rounds * blk * blk,
        ),
        name="pair_first",
    )(shifted, partner)


def pair_kernel(windows, first_ref, *refs):
    shifted, partner_ref = refs[:windows], refs[windows : 2 * windows]
    out_ref, partner_t = refs[2 * windows :]
    rounds, blk, length = partner_ref[0].shape
    scale_two = 1.0 / math.sqrt((windows + 1) * length)
    steps = pl.num_programs(0)
    step = pl.program_id(0)

    @pl.when(step == 0)
    def _():
        for w in range(windows):
            transpose_partners(partner_ref[w], partner_t.at[w])

    top = pl.multiple_of((lax.axis_index("win") * steps + step) * STEP, STEP)
    weights = jnp.concatenate([partner_t[w, pl.ds(top, length), :] for w in range(windows)], axis=0)
    half = blk // 2
    for part in range(2):
        rows = slice(part * half * STEP, (part + 1) * half * STEP)
        samples = jnp.concatenate([shifted[w][rows, :] for w in range(windows)], axis=1)
        result = jnp.dot(samples, weights, preferred_element_type=f32)
        result = ((result + first_ref[0, rows, :]) * scale_two).astype(bf16)
        for r in range(rounds):
            out_ref[r, part * half : (part + 1) * half] = result[:, r * blk : (r + 1) * blk].reshape(
                half, STEP, blk
            )


def pair_coherence(first, shifted, partner, share):
    windows = len(shifted)
    rounds, blk, length = partner[0].shape
    steps = share // STEP
    return pl.pallas_call(
        functools.partial(pair_kernel, windows),
        out_shape=jax.ShapeDtypeStruct((rounds, blk, share, blk), bf16),
        grid=(steps,),
        in_specs=[pl.BlockSpec((1,) + first.shape[1:], lambda step: (step, 0, 0))]
        + [VMEM_SPEC] * (2 * windows),
        out_specs=pl.BlockSpec((rounds, blk, STEP, blk), lambda step: (0, 0, step, 0)),
        scratch_shapes=[pltpu.VMEM((windows, length + LAGS, rounds * blk), bf16)],
        compiler_params=pltpu.CompilerParams(vmem_limit_bytes=20 << 20),
        name="pair_coherence",
    )(first, *shifted, *partner)


def per_device(traces, pairing, aux_owners, coda_start, coda_end):
    win_size = lax.axis_size("win")
    chan_size = lax.axis_size("chan")
    rounds = pairing.shape[0]
    raw = traces[0]

    def exchange(block, k):
        return lax.ppermute(block, "win", [(i, i ^ k) for i in range(win_size)])

    def cross(block):
        return lax.ppermute(block, "chan", [(i, i ^ 1) for i in range(chan_size)])

    column = [raw] + [
        lax.ppermute(raw, "chan", [(i, (i + 2 * k) % chan_size) for i in range(chan_size)])
        for k in range(1, chan_size // 2)
    ]
    own_all = [raw] + [exchange(raw, k) for k in range(1, win_size)]
    shifted = [shifted_copies(block, n == 0) for n, block in enumerate(own_all)]
    column[0] = shifted[0][2]
    copies, own_white = [pair[0] for pair in shifted], [pair[1] for pair in shifted]
    copies, own_white, column = lax.optimization_barrier((copies, own_white, column))
    aux_sent, aux_held, sent, held = pick(aux_owners, pairing, column)
    aux = merge(lambda ref, chan: [ref[0]], aux_owners, aux_held, cross(aux_sent))
    partners = merge(
        lambda ref, chan: [ref[r, chan] for r in range(rounds)], pairing, held, cross(sent)
    )
    aux_rest = [exchange(aux, k) for k in range(1, win_size)]
    pair_begun = pair_first(copies[0], partners, LAGS // win_size)
    part_begun = part_first(aux, own_white[0])
    partners, aux_rest, pair_begun, part_begun = lax.optimization_barrier(
        (partners, aux_rest, pair_begun, part_begun)
    )
    partner_rest = [exchange(partners, k) for k in range(1, win_size)]
    three = coda_coherence(coda_start, coda_end, part_begun, aux_rest, own_white[1:], LAGS3 // win_size)
    pair = pair_coherence(pair_begun, copies[1:], partner_rest, LAGS // win_size)
    return (pair, three)


def solution(mesh):
    in_specs = (P("win", "chan", None), P(), P(), P(), P())
    out_specs = (P(None, "chan", "win", None), P("chan", "win", None))
    return jax.shard_map(per_device, mesh=mesh, in_specs=in_specs, out_specs=out_specs, check_vma=False)
```

```python
import functools
import math

import jax
import jax.numpy as jnp
from jax import lax
from jax.experimental import pallas as pl
from jax.experimental.pallas import tpu as pltpu
from jax.sharding import PartitionSpec as P

LAGS = 256
CODA = 128
CODA_LO = 128
LAGS3 = 128
EPS = 1e-05
STEP = 16
GROUP = 4

SMEM_SPEC = pl.BlockSpec(memory_space=pltpu.SMEM)
VMEM_SPEC = pl.BlockSpec(memory_space=pltpu.VMEM)
ANY_SPEC = pl.BlockSpec(memory_space=pl.ANY)
ROW_PAD = 8
MOVED = 8

f32 = jnp.float32
bf16 = jnp.bfloat16


def white_block(traces):
    samples = traces.astype(f32)
    energy_mean = jnp.mean(samples * samples, axis=-1, keepdims=True)
    return (samples * lax.rsqrt(energy_mean + EPS)).astype(bf16)


def shift_right(block, count):
    if count == 0:
        return block.astype(bf16)
    moved = pltpu.roll(block, count, 1)
    lane = lax.broadcasted_iota(jnp.int32, block.shape, 1)
    return jnp.where(lane < count, 0.0, moved).astype(bf16)


def pick_kernel(rounds, owners_ref, pairing_ref, *refs):
    column, out_refs = refs[:-4], refs[-4:]
    count = len(column)
    chan = lax.axis_index("chan")
    other = chan + 1 - 2 * (chan % 2)
    aux = owners_ref[0]
    slots = [(out_refs[0], aux), (out_refs[1], aux)]
    slots += [(out_refs[2].at[r], pairing_ref[r, other]) for r in range(rounds)]
    slots += [(out_refs[3].at[r], pairing_ref[r, chan]) for r in range(rounds)]
    for slot, block in slots:
        distance = (chan - block + 2 * count) % (2 * count) // 2
        for k in range(count):

            @pl.when(distance == k)
            def _():
                slot[...] = column[k][...]


def pick(owners, pairing, column):
    block = column[0].shape
    rounds = pairing.shape[0]
    shapes = [block, block, (rounds,) + block, (rounds,) + block]
    return pl.pallas_call(
        functools.partial(pick_kernel, rounds),
        out_shape=[jax.ShapeDtypeStruct(shape, bf16) for shape in shapes],
        in_specs=[SMEM_SPEC] * 2 + [VMEM_SPEC] * len(column),
        out_specs=[VMEM_SPEC] * 4,
        compiler_params=pltpu.CompilerParams(vmem_limit_bytes=2 << 20),
        name="pick",
    )(owners, pairing, *column)


def merge(blocks_of, scalars, held, got):
    def kernel(scalars_ref, held_ref, got_ref, out_ref):
        chan = lax.axis_index("chan")
        for r, block in enumerate(blocks_of(scalars_ref, chan)):
            same = (chan + block) % 2 == 0
            here, sent, out = (ref if len(ref.shape) == 2 else ref.at[r] for ref in (held_ref, got_ref, out_ref))

            @pl.when(same)
            def _():
                out[...] = white_block(here[...])

            @pl.when(jnp.logical_not(same))
            def _():
                out[...] = white_block(sent[...])

    return pl.pallas_call(
        kernel,
        out_shape=jax.ShapeDtypeStruct(held.shape, bf16),
        in_specs=[SMEM_SPEC, VMEM_SPEC, VMEM_SPEC],
        out_specs=VMEM_SPEC,
        compiler_params=pltpu.CompilerParams(vmem_limit_bytes=4 << 20),
        name="merge",
    )(scalars, held, got)


def shift_kernel(block_ref, out_ref, white_ref, *raw_ref):
    for ref in raw_ref:
        ref[...] = block_ref[...]
    white_ref[...] = white_block(block_ref[...])
    blk, length = block_ref.shape
    lane = lax.broadcasted_iota(jnp.int32, (STEP, length), 1)
    row = lax.broadcasted_iota(jnp.int32, (STEP, length), 0)
    for i in range(blk):
        samples = jnp.broadcast_to(white_ref[i : i + 1, :].astype(f32), (STEP, length))
        moved = pltpu.roll(samples, 0, 1, stride=1, stride_axis=0)
        out_ref[i * STEP : (i + 1) * STEP, :] = jnp.where(lane < row, 0.0, moved).astype(bf16)


def shifted_copies(block, raw=False):
    blk, length = block.shape
    return pl.pallas_call(
        shift_kernel,
        out_shape=[
            jax.ShapeDtypeStruct((blk * STEP, length), bf16),
            jax.ShapeDtypeStruct((blk, length), bf16),
        ]
        + [jax.ShapeDtypeStruct((blk, length), bf16)] * raw,
        in_specs=[VMEM_SPEC],
        out_specs=[VMEM_SPEC] * (2 + raw),
        compiler_params=pltpu.CompilerParams(vmem_limit_bytes=4 << 20),
        name="shifted_copies",
    )(block)


def part_first_kernel(aux_ref, own_ref, out_ref, shifted, own_t):
    blk, length = own_ref.shape
    used = length - CODA_LO
    step = pl.program_id(0)

    @pl.when(step == 0)
    def _():
        own_t[:length, :] = own_ref[...].T
        own_t[length:, :] = jnp.zeros((own_t.shape[0] - length, blk), bf16)
        samples = aux_ref[...][:, :used].astype(f32)
        for b in range(STEP):
            shifted[b * blk : (b + 1) * blk, :] = shift_right(samples, b)

    halves = [
        own_t[pl.ds(pl.multiple_of(CODA_LO + (2 * step + a) * STEP, STEP), used), :] for a in range(2)
    ]
    out_ref[0] = jnp.dot(shifted[...], jnp.concatenate(halves, axis=1), preferred_element_type=f32)


def part_first(aux, own):
    blk, length = own.shape
    used = length - CODA_LO
    steps = CODA // (2 * STEP)
    return pl.pallas_call(
        part_first_kernel,
        out_shape=jax.ShapeDtypeStruct((steps, STEP * blk, 2 * blk), f32),
        grid=(steps,),
        in_specs=[VMEM_SPEC] * 2,
        out_specs=pl.BlockSpec((1, STEP * blk, 2 * blk), lambda step: (step, 0, 0)),
        scratch_shapes=[pltpu.VMEM((STEP * blk, used), bf16), pltpu.VMEM((length + CODA, blk), bf16)],
        compiler_params=pltpu.CompilerParams(vmem_limit_bytes=16 << 20),
        cost_estimate=pl.CostEstimate(
            flops=2 * CODA * blk * blk * used, transcendentals=0, bytes_accessed=4 * CODA * blk * blk
        ),
        name="part_first",
    )(aux, own)


def coda_kernel(windows, start_ref, end_ref, first, *refs):
    aux_ref, own_ref = refs[:windows], refs[windows : 2 * windows]
    out_ref, moved_ref, shifted, own_t, limits, coda, coda_t, acc, rows = refs[2 * windows :]
    blk, length = own_ref[0].shape
    used = length - CODA_LO
    share = out_ref.shape[1]
    steps = share // 2
    pairs = CODA // 2
    scale_two = 1.0 / math.sqrt((windows + 1) * length)
    scale_three = 1.0 / math.sqrt(blk * CODA)
    win = lax.axis_index("win")

    limits[0] = jnp.broadcast_to(start_ref[...], (blk, blk)).T
    limits[1] = jnp.broadcast_to(end_ref[...], (blk, blk)).T
    for w in range(windows):
        own_t[w, :length, :] = own_ref[w][...].T
        own_t[w, length:, :] = jnp.zeros((own_t.shape[1] - length, blk), bf16)
        samples = aux_ref[w][:, :used].astype(f32)
        for b in range(STEP):
            shifted[b * blk : (b + 1) * blk, w * used : (w + 1) * used] = shift_right(samples, b)
    coda[CODA * blk :, :] = jnp.zeros((coda.shape[0] - CODA * blk, blk), bf16)
    coda_t[: (steps - 1) * blk, :] = jnp.zeros(((steps - 1) * blk, 2 * blk), bf16)

    chunk = STEP // 2

    def part(a_pair, limit):
        pieces = []
        for w in range(windows):
            halves = [
                own_t[w, pl.ds(pl.multiple_of(CODA_LO + (2 * a_pair + a) * STEP, STEP), used), :]
                for a in range(2)
            ]
            pieces.append(jnp.concatenate(halves, axis=1))
        weights = jnp.concatenate(pieces, axis=0)
        for b_first in range(0, STEP, chunk):
            rows_here = slice(b_first * blk, (b_first + chunk) * blk)
            result = jnp.dot(shifted[rows_here, :], weights, preferred_element_type=f32)
            result = (result + first[a_pair, rows_here, :]) * scale_two
            for b in range(chunk):
                for a in range(2):
                    lag = (2 * a_pair + a) * STEP + b_first + b
                    tile = result[b * blk : (b + 1) * blk, a * blk : (a + 1) * blk]
                    if limit == 0:
                        tile = jnp.where(lag >= limits[0], tile, 0.0)
                    if limit == 1:
                        tile = jnp.where(lag < limits[1], tile, 0.0)
                    tile = tile.astype(bf16)
                    coda[pl.ds(pl.multiple_of(lag * blk, blk), blk), :] = tile
                    place = pl.multiple_of((lag // 2 + steps - 1) * blk, blk)
                    coda_t[pl.ds(place, blk), (b % 2) * blk : (b % 2 + 1) * blk] = tile.T

    def run(first_step, last_step, limit):
        def body(step, _):
            part(step, limit)
            return 0

        lax.fori_loop(first_step, last_step, body, 0)

    count = CODA // (2 * STEP)
    run(0, count // 4, 0)
    run(count // 4, 3 * count // 4, None)
    run(3 * count // 4, count, 1)

    def accumulate(group, size, blocks, lag_first, total):
        lhs, rhs = [], []
        for q in range(size):
            pair = group * size + q
            row = (pair + steps - blocks) * blk
            lhs.append(coda_t[pl.ds(pl.multiple_of(row, blk), blocks * blk), :])
            top = (2 * pair + lag_first) * blk
            rhs.append(
                jnp.concatenate(
                    [coda[pl.ds(pl.multiple_of(top + b * blk, blk), 2 * blk), :] for b in range(2)], axis=1
                )
            )
        value = jnp.dot(
            jnp.concatenate(lhs, axis=1), jnp.concatenate(rhs, axis=0), preferred_element_type=f32
        )
        acc[(total - blocks) * blk : total * blk, :] += value

    def correlate(lag_first, total, target_ref, size=GROUP):
        acc[: total * blk, :] = jnp.zeros((total * blk, acc.shape[1]), f32)
        peeled = total // size - 1
        for group in range(peeled):
            accumulate(group, size, (group + 1) * size, lag_first, total)

        def whole(group, _):
            accumulate(group, size, total, lag_first, total)
            return 0

        lax.fori_loop(max(peeled, 0), (pairs - lag_first // 2 + size - 1) // size, whole, 0)
        stride = 2 * total + ROW_PAD
        for i in range(total):
            for b in range(2):
                lag = 2 * (total - 1 - i) + b
                rows[pl.ds(lag, blk, stride=stride), :] = (
                    acc[i * blk : (i + 1) * blk, b * blk : (b + 1) * blk] * scale_three
                )
        target_ref[:, : 2 * total, :] = (
            rows[: blk * stride].reshape(blk, stride, blk)[:, : 2 * total].astype(bf16)
        )

    last = lax.axis_size("win") - 1

    @pl.when(win > 0)
    def _():
        correlate(win * share, steps, out_ref)

    kept = share // 2

    @pl.when(win == 0)
    def _():
        correlate(0, kept // 2, out_ref)

    @pl.when(win > last - kept // MOVED)
    def _():
        correlate(kept + MOVED * (last - win), MOVED // 2, moved_ref, 2 * GROUP)


def finish_kernel(count, *refs):
    moved_refs, (_, out_ref, sems) = refs[:count], refs[count:]
    kept = out_ref.shape[1] - MOVED * count

    @pl.when(lax.axis_index("win") == 0)
    def _():
        copies = [
            pltpu.make_async_copy(moved, out_ref.at[:, kept + MOVED * n : kept + MOVED * (n + 1), :], sems.at[n])
            for n, moved in enumerate(moved_refs)
        ]
        for copy in copies:
            copy.start()
        for copy in copies:
            copy.wait()


def finish(moved, three):
    count = len(moved)
    return pl.pallas_call(
        functools.partial(finish_kernel, count),
        out_shape=jax.ShapeDtypeStruct(three.shape, bf16),
        in_specs=[ANY_SPEC] * (count + 1),
        out_specs=ANY_SPEC,
        scratch_shapes=[pltpu.SemaphoreType.DMA((count,))],
        input_output_aliases={count: 0},
        compiler_params=pltpu.CompilerParams(vmem_limit_bytes=1 << 20),
        name="finish",
    )(*moved, three)


def coda_limit(windows, blk, used):
    return (21 << 20) + 2 * STEP * blk * windows * used


def coda_coherence(start, end, first, aux, own, share):
    windows = len(own)
    blk, length = own[0].shape
    used = length - CODA_LO
    steps = share // 2
    return pl.pallas_call(
        functools.partial(coda_kernel, windows),
        out_shape=[
            jax.ShapeDtypeStruct((blk, share, blk), bf16),
            jax.ShapeDtypeStruct((blk, MOVED, blk), bf16),
        ],
        in_specs=[VMEM_SPEC] * (3 + 2 * windows),
        out_specs=[VMEM_SPEC] * 2,
        scratch_shapes=[
            pltpu.VMEM((STEP * blk, windows * used), bf16),
            pltpu.VMEM((windows, length + CODA, blk), bf16),
            pltpu.VMEM((2, blk, blk), jnp.int32),
            pltpu.VMEM(((CODA + 4 * GROUP) * blk, blk), bf16),
            pltpu.VMEM(((CODA // 2 + steps - 1) * blk, 2 * blk), bf16),
            pltpu.VMEM((steps * blk, 2 * blk), f32),
            pltpu.VMEM(((share + ROW_PAD) * blk, blk), f32),
        ],
        compiler_params=pltpu.CompilerParams(vmem_limit_bytes=coda_limit(windows, blk, used)),
        cost_estimate=pl.CostEstimate(
            flops=2 * CODA * blk * blk * (windows * used + blk * share), transcendentals=0, bytes_accessed=16 << 20
        ),
        name="coda_coherence",
    )(start, end, first, *aux, *own)


def transpose_partners(partner_ref, partner_t):
    rounds, blk, length = partner_ref.shape
    for r in range(rounds):
        partner_t[:length, r * blk : (r + 1) * blk] = partner_ref[r].T
    partner_t[length:, :] = jnp.zeros((partner_t.shape[0] - length, rounds * blk), bf16)


def pair_first_kernel(shifted_ref, partner_ref, out_ref, partner_t):
    length = partner_ref.shape[2]
    steps = pl.num_programs(0)
    step = pl.program_id(0)

    @pl.when(step == 0)
    def _():
        transpose_partners(partner_ref, partner_t)

    top = pl.multiple_of((lax.axis_index("win") * steps + step) * STEP, STEP)
    out_ref[0] = jnp.dot(shifted_ref[...], partner_t[pl.ds(top, length), :], preferred_element_type=f32)


def pair_first(shifted, partner, share):
    rounds, blk, length = partner.shape
    steps = share // STEP
    return pl.pallas_call(
        pair_first_kernel,
        out_shape=jax.ShapeDtypeStruct((steps, blk * STEP, rounds * blk), f32),
        grid=(steps,),
        in_specs=[VMEM_SPEC, VMEM_SPEC],
        out_specs=pl.BlockSpec((1, blk * STEP, rounds * blk), lambda step: (step, 0, 0)),
        scratch_shapes=[pltpu.VMEM((length + LAGS, rounds * blk), bf16)],
        compiler_params=pltpu.CompilerParams(vmem_limit_bytes=12 << 20),
        cost_estimate=pl.CostEstimate(
            flops=2 * share * rounds * blk * blk * length,
            transcendentals=0,
            bytes_accessed=4 * share * rounds * blk * blk,
        ),
        name="pair_first",
    )(shifted, partner)


def pair_kernel(windows, first_ref, *refs):
    shifted, partner_ref = refs[:windows], refs[windows : 2 * windows]
    out_ref, partner_t = refs[2 * windows :]
    rounds, blk, length = partner_ref[0].shape
    scale_two = 1.0 / math.sqrt((windows + 1) * length)
    steps = pl.num_programs(0)
    step = pl.program_id(0)

    @pl.when(step == 0)
    def _():
        for w in range(windows):
            transpose_partners(partner_ref[w], partner_t.at[w])

    top = pl.multiple_of((lax.axis_index("win") * steps + step) * STEP, STEP)
    weights = jnp.concatenate([partner_t[w, pl.ds(top, length), :] for w in range(windows)], axis=0)
    half = blk // 2
    for part in range(2):
        rows = slice(part * half * STEP, (part + 1) * half * STEP)
        samples = jnp.concatenate([shifted[w][rows, :] for w in range(windows)], axis=1)
        result = jnp.dot(samples, weights, preferred_element_type=f32)
        result = ((result + first_ref[0, rows, :]) * scale_two).astype(bf16)
        for r in range(rounds):
            out_ref[r, part * half : (part + 1) * half] = result[:, r * blk : (r + 1) * blk].reshape(
                half, STEP, blk
            )


def pair_coherence(first, shifted, partner, share):
    windows = len(shifted)
    rounds, blk, length = partner[0].shape
    steps = share // STEP
    return pl.pallas_call(
        functools.partial(pair_kernel, windows),
        out_shape=jax.ShapeDtypeStruct((rounds, blk, share, blk), bf16),
        grid=(steps,),
        in_specs=[pl.BlockSpec((1,) + first.shape[1:], lambda step: (step, 0, 0))]
        + [VMEM_SPEC] * (2 * windows),
        out_specs=pl.BlockSpec((rounds, blk, STEP, blk), lambda step: (0, 0, step, 0)),
        scratch_shapes=[pltpu.VMEM((windows, length + LAGS, rounds * blk), bf16)],
        compiler_params=pltpu.CompilerParams(vmem_limit_bytes=20 << 20),
        cost_estimate=pl.CostEstimate(
            flops=2 * rounds * share * blk * blk * windows * length, transcendentals=0, bytes_accessed=16 << 20
        ),
        name="pair_coherence",
    )(first, *shifted, *partner)


def per_device(traces, pairing, aux_owners, coda_start, coda_end):
    win_size = lax.axis_size("win")
    chan_size = lax.axis_size("chan")
    rounds = pairing.shape[0]
    raw = traces[0]

    def exchange(block, k):
        return lax.ppermute(block, "win", [(i, i ^ k) for i in range(win_size)])

    def cross(block):
        return lax.ppermute(block, "chan", [(i, i ^ 1) for i in range(chan_size)])

    column = [raw] + [
        lax.ppermute(raw, "chan", [(i, (i + 2 * k) % chan_size) for i in range(chan_size)])
        for k in range(1, chan_size // 2)
    ]
    own_all = [raw] + [exchange(raw, k) for k in range(1, win_size)]
    shifted = [shifted_copies(block, n == 0) for n, block in enumerate(own_all)]
    column[0] = shifted[0][2]
    copies, own_white = [pair[0] for pair in shifted], [pair[1] for pair in shifted]
    copies, own_white, column = lax.optimization_barrier((copies, own_white, column))
    aux_sent, aux_held, sent, held = pick(aux_owners, pairing, column)
    aux = merge(lambda ref, chan: [ref[0]], aux_owners, aux_held, cross(aux_sent))
    partners = merge(
        lambda ref, chan: [ref[r, chan] for r in range(rounds)], pairing, held, cross(sent)
    )
    aux_rest = [exchange(aux, k) for k in range(1, win_size)]
    pair_begun = pair_first(copies[0], partners, LAGS // win_size)
    part_begun = part_first(aux, own_white[0])
    partners, aux_rest, pair_begun, part_begun = lax.optimization_barrier(
        (partners, aux_rest, pair_begun, part_begun)
    )
    partner_rest = [exchange(partners, k) for k in range(1, win_size)]
    three, moved = coda_coherence(coda_start, coda_end, part_begun, aux_rest, own_white[1:], LAGS3 // win_size)
    pair = pair_coherence(pair_begun, copies[1:], partner_rest, LAGS // win_size)
    helpers = LAGS3 // win_size // 2 // MOVED
    moved = [lax.ppermute(moved, "win", [(win_size - 1 - n, 0)]) for n in range(helpers)]
    pair, three, moved = lax.optimization_barrier((pair, three, moved))
    return (pair, finish(moved, three))


def solution(mesh):
    in_specs = (P("win", "chan", None), P(), P(), P(), P())
    out_specs = (P(None, "chan", "win", None), P("chan", "win", None))
    return jax.shard_map(per_device, mesh=mesh, in_specs=in_specs, out_specs=out_specs, check_vma=False)
```

```python
import functools
import math

import jax
import jax.numpy as jnp
from jax import lax
from jax.experimental import pallas as pl
from jax.experimental.pallas import tpu as pltpu
from jax.sharding import PartitionSpec as P

LAGS = 256
CODA = 128
CODA_LO = 128
LAGS3 = 128
EPS = 1e-05
STEP = 16
GROUP = 4

SMEM_SPEC = pl.BlockSpec(memory_space=pltpu.SMEM)
VMEM_SPEC = pl.BlockSpec(memory_space=pltpu.VMEM)
ANY_SPEC = pl.BlockSpec(memory_space=pl.ANY)
ROW_PAD = 8
MOVED = 8

f32 = jnp.float32
bf16 = jnp.bfloat16


def white_block(traces):
    samples = traces.astype(f32)
    energy_mean = jnp.mean(samples * samples, axis=-1, keepdims=True)
    return (samples * lax.rsqrt(energy_mean + EPS)).astype(bf16)


def shift_right(block, count):
    if count == 0:
        return block.astype(bf16)
    moved = pltpu.roll(block, count, 1)
    lane = lax.broadcasted_iota(jnp.int32, block.shape, 1)
    return jnp.where(lane < count, 0.0, moved).astype(bf16)


def pick_kernel(rounds, owners_ref, pairing_ref, *refs):
    column, out_refs = refs[:-4], refs[-4:]
    count = len(column)
    chan = lax.axis_index("chan")
    other = chan + 1 - 2 * (chan % 2)
    aux = owners_ref[0]
    slots = [(out_refs[0], aux), (out_refs[1], aux)]
    slots += [(out_refs[2].at[r], pairing_ref[r, other]) for r in range(rounds)]
    slots += [(out_refs[3].at[r], pairing_ref[r, chan]) for r in range(rounds)]
    for slot, block in slots:
        distance = (chan - block + 2 * count) % (2 * count) // 2
        for k in range(count):

            @pl.when(distance == k)
            def _():
                slot[...] = column[k][...]


def pick(owners, pairing, column):
    block = column[0].shape
    rounds = pairing.shape[0]
    shapes = [block, block, (rounds,) + block, (rounds,) + block]
    return pl.pallas_call(
        functools.partial(pick_kernel, rounds),
        out_shape=[jax.ShapeDtypeStruct(shape, bf16) for shape in shapes],
        in_specs=[SMEM_SPEC] * 2 + [VMEM_SPEC] * len(column),
        out_specs=[VMEM_SPEC] * 4,
        compiler_params=pltpu.CompilerParams(vmem_limit_bytes=2 << 20),
        cost_estimate=pl.CostEstimate(flops=0, transcendentals=0, bytes_accessed=1<<20),
        name="pick",
    )(owners, pairing, *column)


def merge(blocks_of, scalars, held, got):
    def kernel(scalars_ref, held_ref, got_ref, out_ref):
        chan = lax.axis_index("chan")
        for r, block in enumerate(blocks_of(scalars_ref, chan)):
            same = (chan + block) % 2 == 0
            here, sent, out = (ref if len(ref.shape) == 2 else ref.at[r] for ref in (held_ref, got_ref, out_ref))

            @pl.when(same)
            def _():
                out[...] = white_block(here[...])

            @pl.when(jnp.logical_not(same))
            def _():
                out[...] = white_block(sent[...])

    return pl.pallas_call(
        kernel,
        out_shape=jax.ShapeDtypeStruct(held.shape, bf16),
        in_specs=[SMEM_SPEC, VMEM_SPEC, VMEM_SPEC],
        out_specs=VMEM_SPEC,
        compiler_params=pltpu.CompilerParams(vmem_limit_bytes=4 << 20),
        cost_estimate=pl.CostEstimate(flops=0, transcendentals=0, bytes_accessed=1<<20),
        name="merge",
    )(scalars, held, got)


def shift_kernel(block_ref, out_ref, white_ref, *raw_ref):
    for ref in raw_ref:
        ref[...] = block_ref[...]
    white_ref[...] = white_block(block_ref[...])
    blk, length = block_ref.shape
    lane = lax.broadcasted_iota(jnp.int32, (STEP, length), 1)
    row = lax.broadcasted_iota(jnp.int32, (STEP, length), 0)
    for i in range(blk):
        samples = jnp.broadcast_to(white_ref[i : i + 1, :].astype(f32), (STEP, length))
        moved = pltpu.roll(samples, 0, 1, stride=1, stride_axis=0)
        out_ref[i * STEP : (i + 1) * STEP, :] = jnp.where(lane < row, 0.0, moved).astype(bf16)


def shifted_copies(block, raw=False):
    blk, length = block.shape
    return pl.pallas_call(
        shift_kernel,
        out_shape=[
            jax.ShapeDtypeStruct((blk * STEP, length), bf16),
            jax.ShapeDtypeStruct((blk, length), bf16),
        ]
        + [jax.ShapeDtypeStruct((blk, length), bf16)] * raw,
        in_specs=[VMEM_SPEC],
        out_specs=[VMEM_SPEC] * (2 + raw),
        compiler_params=pltpu.CompilerParams(vmem_limit_bytes=4 << 20),
        cost_estimate=pl.CostEstimate(flops=0, transcendentals=0, bytes_accessed=3<<20),
        name="shifted_copies",
    )(block)


def part_first_kernel(aux_ref, own_ref, out_ref, shifted, own_t):
    blk, length = own_ref.shape
    used = length - CODA_LO
    step = pl.program_id(0)

    @pl.when(step == 0)
    def _():
        own_t[:length, :] = own_ref[...].T
        own_t[length:, :] = jnp.zeros((own_t.shape[0] - length, blk), bf16)
        samples = aux_ref[...][:, :used].astype(f32)
        for b in range(STEP):
            shifted[b * blk : (b + 1) * blk, :] = shift_right(samples, b)

    halves = [
        own_t[pl.ds(pl.multiple_of(CODA_LO + (2 * step + a) * STEP, STEP), used), :] for a in range(2)
    ]
    out_ref[0] = jnp.dot(shifted[...], jnp.concatenate(halves, axis=1), preferred_element_type=f32)


def part_first(aux, own):
    blk, length = own.shape
    used = length - CODA_LO
    steps = CODA // (2 * STEP)
    return pl.pallas_call(
        part_first_kernel,
        out_shape=jax.ShapeDtypeStruct((steps, STEP * blk, 2 * blk), f32),
        grid=(steps,),
        in_specs=[VMEM_SPEC] * 2,
        out_specs=pl.BlockSpec((1, STEP * blk, 2 * blk), lambda step: (step, 0, 0)),
        scratch_shapes=[pltpu.VMEM((STEP * blk, used), bf16), pltpu.VMEM((length + CODA, blk), bf16)],
        compiler_params=pltpu.CompilerParams(vmem_limit_bytes=16 << 20),
        cost_estimate=pl.CostEstimate(
            flops=2 * CODA * blk * blk * used, transcendentals=0, bytes_accessed=4 * CODA * blk * blk
        ),
        name="part_first",
    )(aux, own)


def coda_kernel(windows, start_ref, end_ref, first, *refs):
    aux_ref, own_ref = refs[:windows], refs[windows : 2 * windows]
    out_ref, moved_ref, shifted, own_t, limits, coda, coda_t, acc, rows = refs[2 * windows :]
    blk, length = own_ref[0].shape
    used = length - CODA_LO
    share = out_ref.shape[1]
    steps = share // 2
    pairs = CODA // 2
    scale_two = 1.0 / math.sqrt((windows + 1) * length)
    scale_three = 1.0 / math.sqrt(blk * CODA)
    win = lax.axis_index("win")

    limits[0] = jnp.broadcast_to(start_ref[...], (blk, blk)).T
    limits[1] = jnp.broadcast_to(end_ref[...], (blk, blk)).T
    for w in range(windows):
        own_t[w, :length, :] = own_ref[w][...].T
        own_t[w, length:, :] = jnp.zeros((own_t.shape[1] - length, blk), bf16)
        samples = aux_ref[w][:, :used].astype(f32)
        for b in range(STEP):
            shifted[b * blk : (b + 1) * blk, w * used : (w + 1) * used] = shift_right(samples, b)
    coda[CODA * blk :, :] = jnp.zeros((coda.shape[0] - CODA * blk, blk), bf16)
    coda_t[: (steps - 1) * blk, :] = jnp.zeros(((steps - 1) * blk, 2 * blk), bf16)

    chunk = STEP // 2

    def part(a_pair, limit):
        pieces = []
        for w in range(windows):
            halves = [
                own_t[w, pl.ds(pl.multiple_of(CODA_LO + (2 * a_pair + a) * STEP, STEP), used), :]
                for a in range(2)
            ]
            pieces.append(jnp.concatenate(halves, axis=1))
        weights = jnp.concatenate(pieces, axis=0)
        for b_first in range(0, STEP, chunk):
            rows_here = slice(b_first * blk, (b_first + chunk) * blk)
            result = jnp.dot(shifted[rows_here, :], weights, preferred_element_type=f32)
            result = (result + first[a_pair, rows_here, :]) * scale_two
            for b in range(chunk):
                for a in range(2):
                    lag = (2 * a_pair + a) * STEP + b_first + b
                    tile = result[b * blk : (b + 1) * blk, a * blk : (a + 1) * blk]
                    if limit == 0:
                        tile = jnp.where(lag >= limits[0], tile, 0.0)
                    if limit == 1:
                        tile = jnp.where(lag < limits[1], tile, 0.0)
                    tile = tile.astype(bf16)
                    coda[pl.ds(pl.multiple_of(lag * blk, blk), blk), :] = tile
                    place = pl.multiple_of((lag // 2 + steps - 1) * blk, blk)
                    coda_t[pl.ds(place, blk), (b % 2) * blk : (b % 2 + 1) * blk] = tile.T

    def run(first_step, last_step, limit):
        def body(step, _):
            part(step, limit)
            return 0

        lax.fori_loop(first_step, last_step, body, 0)

    count = CODA // (2 * STEP)
    run(0, count // 4, 0)
    run(count // 4, 3 * count // 4, None)
    run(3 * count // 4, count, 1)

    def accumulate(group, size, blocks, lag_first, total):
        lhs, rhs = [], []
        for q in range(size):
            pair = group * size + q
            row = (pair + steps - blocks) * blk
            lhs.append(coda_t[pl.ds(pl.multiple_of(row, blk), blocks * blk), :])
            top = (2 * pair + lag_first) * blk
            rhs.append(
                jnp.concatenate(
                    [coda[pl.ds(pl.multiple_of(top + b * blk, blk), 2 * blk), :] for b in range(2)], axis=1
                )
            )
        value = jnp.dot(
            jnp.concatenate(lhs, axis=1), jnp.concatenate(rhs, axis=0), preferred_element_type=f32
        )
        acc[(total - blocks) * blk : total * blk, :] += value

    def correlate(lag_first, total, target_ref, size=GROUP):
        acc[: total * blk, :] = jnp.zeros((total * blk, acc.shape[1]), f32)
        peeled = total // size - 1
        for group in range(peeled):
            accumulate(group, size, (group + 1) * size, lag_first, total)

        def whole(group, _):
            accumulate(group, size, total, lag_first, total)
            return 0

        lax.fori_loop(max(peeled, 0), (pairs - lag_first // 2 + size - 1) // size, whole, 0)
        stride = 2 * total + ROW_PAD
        for i in range(total):
            for b in range(2):
                lag = 2 * (total - 1 - i) + b
                rows[pl.ds(lag, blk, stride=stride), :] = (
                    acc[i * blk : (i + 1) * blk, b * blk : (b + 1) * blk] * scale_three
                )
        target_ref[:, : 2 * total, :] = (
            rows[: blk * stride].reshape(blk, stride, blk)[:, : 2 * total].astype(bf16)
        )

    last = lax.axis_size("win") - 1

    @pl.when(win > 0)
    def _():
        correlate(win * share, steps, out_ref)

    kept = share // 2

    @pl.when(win == 0)
    def _():
        correlate(0, kept // 2, out_ref)

    @pl.when(win > last - kept // MOVED)
    def _():
        correlate(kept + MOVED * (last - win), MOVED // 2, moved_ref, 2 * GROUP)


def finish_kernel(count, *refs):
    moved_refs, (_, out_ref, sems) = refs[:count], refs[count:]
    kept = out_ref.shape[1] - MOVED * count

    @pl.when(lax.axis_index("win") == 0)
    def _():
        copies = [
            pltpu.make_async_copy(moved, out_ref.at[:, kept + MOVED * n : kept + MOVED * (n + 1), :], sems.at[n])
            for n, moved in enumerate(moved_refs)
        ]
        for copy in copies:
            copy.start()
        for copy in copies:
            copy.wait()


def finish(moved, three):
    count = len(moved)
    return pl.pallas_call(
        functools.partial(finish_kernel, count),
        out_shape=jax.ShapeDtypeStruct(three.shape, bf16),
        in_specs=[ANY_SPEC] * (count + 1),
        out_specs=ANY_SPEC,
        scratch_shapes=[pltpu.SemaphoreType.DMA((count,))],
        input_output_aliases={count: 0},
        compiler_params=pltpu.CompilerParams(vmem_limit_bytes=1 << 20),
        name="finish",
    )(*moved, three)


def coda_limit(windows, blk, used):
    return (21 << 20) + 2 * STEP * blk * windows * used


def coda_coherence(start, end, first, aux, own, share):
    windows = len(own)
    blk, length = own[0].shape
    used = length - CODA_LO
    steps = share // 2
    return pl.pallas_call(
        functools.partial(coda_kernel, windows),
        out_shape=[
            jax.ShapeDtypeStruct((blk, share, blk), bf16),
            jax.ShapeDtypeStruct((blk, MOVED, blk), bf16),
        ],
        in_specs=[VMEM_SPEC] * (3 + 2 * windows),
        out_specs=[VMEM_SPEC] * 2,
        scratch_shapes=[
            pltpu.VMEM((STEP * blk, windows * used), bf16),
            pltpu.VMEM((windows, length + CODA, blk), bf16),
            pltpu.VMEM((2, blk, blk), jnp.int32),
            pltpu.VMEM(((CODA + 4 * GROUP) * blk, blk), bf16),
            pltpu.VMEM(((CODA // 2 + steps - 1) * blk, 2 * blk), bf16),
            pltpu.VMEM((steps * blk, 2 * blk), f32),
            pltpu.VMEM(((share + ROW_PAD) * blk, blk), f32),
        ],
        compiler_params=pltpu.CompilerParams(vmem_limit_bytes=coda_limit(windows, blk, used)),
        cost_estimate=pl.CostEstimate(
            flops=2 * CODA * blk * blk * (windows * used + blk * share), transcendentals=0, bytes_accessed=16 << 20
        ),
        name="coda_coherence",
    )(start, end, first, *aux, *own)


def transpose_partners(partner_ref, partner_t):
    rounds, blk, length = partner_ref.shape
    for r in range(rounds):
        partner_t[:length, r * blk : (r + 1) * blk] = partner_ref[r].T
    partner_t[length:, :] = jnp.zeros((partner_t.shape[0] - length, rounds * blk), bf16)


def pair_first_kernel(shifted_ref, partner_ref, out_ref, partner_t):
    length = partner_ref.shape[2]
    steps = pl.num_programs(0)
    step = pl.program_id(0)

    @pl.when(step == 0)
    def _():
        transpose_partners(partner_ref, partner_t)

    top = pl.multiple_of((lax.axis_index("win") * steps + step) * STEP, STEP)
    out_ref[0] = jnp.dot(shifted_ref[...], partner_t[pl.ds(top, length), :], preferred_element_type=f32)


def pair_first(shifted, partner, share):
    rounds, blk, length = partner.shape
    steps = share // STEP
    return pl.pallas_call(
        pair_first_kernel,
        out_shape=jax.ShapeDtypeStruct((steps, blk * STEP, rounds * blk), f32),
        grid=(steps,),
        in_specs=[VMEM_SPEC, VMEM_SPEC],
        out_specs=pl.BlockSpec((1, blk * STEP, rounds * blk), lambda step: (step, 0, 0)),
        scratch_shapes=[pltpu.VMEM((length + LAGS, rounds * blk), bf16)],
        compiler_params=pltpu.CompilerParams(vmem_limit_bytes=12 << 20),
        cost_estimate=pl.CostEstimate(
            flops=2 * share * rounds * blk * blk * length,
            transcendentals=0,
            bytes_accessed=4 * share * rounds * blk * blk,
        ),
        name="pair_first",
    )(shifted, partner)


def pair_kernel(windows, first_ref, *refs):
    shifted, partner_ref = refs[:windows], refs[windows : 2 * windows]
    out_ref, partner_t = refs[2 * windows :]
    rounds, blk, length = partner_ref[0].shape
    scale_two = 1.0 / math.sqrt((windows + 1) * length)
    steps = pl.num_programs(0)
    step = pl.program_id(0)

    @pl.when(step == 0)
    def _():
        for w in range(windows):
            transpose_partners(partner_ref[w], partner_t.at[w])

    top = pl.multiple_of((lax.axis_index("win") * steps + step) * STEP, STEP)
    weights = jnp.concatenate([partner_t[w, pl.ds(top, length), :] for w in range(windows)], axis=0)
    half = blk // 2
    for part in range(2):
        rows = slice(part * half * STEP, (part + 1) * half * STEP)
        samples = jnp.concatenate([shifted[w][rows, :] for w in range(windows)], axis=1)
        result = jnp.dot(samples, weights, preferred_element_type=f32)
        result = ((result + first_ref[0, rows, :]) * scale_two).astype(bf16)
        for r in range(rounds):
            out_ref[r, part * half : (part + 1) * half] = result[:, r * blk : (r + 1) * blk].reshape(
                half, STEP, blk
            )


def pair_coherence(first, shifted, partner, share):
    windows = len(shifted)
    rounds, blk, length = partner[0].shape
    steps = share // STEP
    return pl.pallas_call(
        functools.partial(pair_kernel, windows),
        out_shape=jax.ShapeDtypeStruct((rounds, blk, share, blk), bf16),
        grid=(steps,),
        in_specs=[pl.BlockSpec((1,) + first.shape[1:], lambda step: (step, 0, 0))]
        + [VMEM_SPEC] * (2 * windows),
        out_specs=pl.BlockSpec((rounds, blk, STEP, blk), lambda step: (0, 0, step, 0)),
        scratch_shapes=[pltpu.VMEM((windows, length + LAGS, rounds * blk), bf16)],
        compiler_params=pltpu.CompilerParams(vmem_limit_bytes=20 << 20),
        cost_estimate=pl.CostEstimate(
            flops=2 * rounds * share * blk * blk * windows * length, transcendentals=0, bytes_accessed=16 << 20
        ),
        name="pair_coherence",
    )(first, *shifted, *partner)


def per_device(traces, pairing, aux_owners, coda_start, coda_end):
    win_size = lax.axis_size("win")
    chan_size = lax.axis_size("chan")
    rounds = pairing.shape[0]
    raw = traces[0]

    def exchange(block, k):
        return lax.ppermute(block, "win", [(i, i ^ k) for i in range(win_size)])

    def cross(block):
        return lax.ppermute(block, "chan", [(i, i ^ 1) for i in range(chan_size)])

    column = [raw] + [
        lax.ppermute(raw, "chan", [(i, (i + 2 * k) % chan_size) for i in range(chan_size)])
        for k in range(1, chan_size // 2)
    ]
    own_rest = [exchange(raw, k) for k in range(1, win_size)]
    first_copies, own_white, column[0] = shifted_copies(raw, True)
    early = [shifted_copies(block) for block in own_rest[:2]]
    first_copies, own_white, early, column = lax.optimization_barrier((first_copies, own_white, early, column))
    aux_sent, aux_held, sent, held = pick(aux_owners, pairing, column)
    aux_sent, sent, own_rest = lax.optimization_barrier((aux_sent, sent, own_rest[2:]))
    shifted = early + [shifted_copies(block) for block in own_rest]
    copies, own_rest = [both[0] for both in shifted], [both[1] for both in shifted]
    aux = merge(lambda ref, chan: [ref[0]], aux_owners, aux_held, cross(aux_sent))
    partners = merge(
        lambda ref, chan: [ref[r, chan] for r in range(rounds)], pairing, held, cross(sent)
    )
    aux_rest = [exchange(aux, k) for k in range(1, win_size)]
    pair_begun = pair_first(first_copies, partners, LAGS // win_size)
    part_begun = part_first(aux, own_white)
    partners, aux_rest, pair_begun, part_begun, copies = lax.optimization_barrier(
        (partners, aux_rest, pair_begun, part_begun, copies)
    )
    partner_rest = [exchange(partners, k) for k in range(1, win_size)]
    three, moved = coda_coherence(coda_start, coda_end, part_begun, aux_rest, own_rest, LAGS3 // win_size)
    pair = pair_coherence(pair_begun, copies, partner_rest, LAGS // win_size)
    helpers = LAGS3 // win_size // 2 // MOVED
    moved = [lax.ppermute(moved, "win", [(win_size - 1 - n, 0)]) for n in range(helpers)]
    pair, three, moved = lax.optimization_barrier((pair, three, moved))
    return (pair, finish(moved, three))


def solution(mesh):
    in_specs = (P("win", "chan", None), P(), P(), P(), P())
    out_specs = (P(None, "chan", "win", None), P("chan", "win", None))
    return jax.shard_map(per_device, mesh=mesh, in_specs=in_specs, out_specs=out_specs, check_vma=False)
```

```python
import functools
import math

import jax
import jax.numpy as jnp
from jax import lax
from jax.experimental import pallas as pl
from jax.experimental.pallas import tpu as pltpu
from jax.sharding import PartitionSpec as P

LAGS = 256
CODA = 128
CODA_LO = 128
LAGS3 = 128
EPS = 1e-05
STEP = 16
GROUP = 4

SMEM_SPEC = pl.BlockSpec(memory_space=pltpu.SMEM)
VMEM_SPEC = pl.BlockSpec(memory_space=pltpu.VMEM)
ANY_SPEC = pl.BlockSpec(memory_space=pl.ANY)
ROW_PAD = 8
MOVED = 8

f32 = jnp.float32
bf16 = jnp.bfloat16


def white_block(traces):
    samples = traces.astype(f32)
    energy_mean = jnp.mean(samples * samples, axis=-1, keepdims=True)
    return (samples * lax.rsqrt(energy_mean + EPS)).astype(bf16)


def shift_right(block, count):
    if count == 0:
        return block.astype(bf16)
    moved = pltpu.roll(block, count, 1)
    lane = lax.broadcasted_iota(jnp.int32, block.shape, 1)
    return jnp.where(lane < count, 0.0, moved).astype(bf16)


def pick_kernel(rounds, owners_ref, pairing_ref, *refs):
    column, out_refs = refs[:-4], refs[-4:]
    count = len(column)
    chan = lax.axis_index("chan")
    other = chan + 1 - 2 * (chan % 2)
    aux = owners_ref[0]
    slots = [(out_refs[0], aux), (out_refs[1], aux)]
    slots += [(out_refs[2].at[r], pairing_ref[r * 2 * count + other]) for r in range(rounds)]
    slots += [(out_refs[3].at[r], pairing_ref[r * 2 * count + chan]) for r in range(rounds)]
    for slot, block in slots:
        distance = (chan - block + 2 * count) % (2 * count) // 2
        for k in range(count):

            @pl.when(distance == k)
            def _():
                slot[...] = column[k][...]


def pick(owners, pairing, column):
    block = column[0].shape
    rounds = pairing.shape[0] // (2 * len(column))
    shapes = [block, block, (rounds,) + block, (rounds,) + block]
    return pl.pallas_call(
        functools.partial(pick_kernel, rounds),
        out_shape=[jax.ShapeDtypeStruct(shape, bf16) for shape in shapes],
        in_specs=[SMEM_SPEC] * 2 + [VMEM_SPEC] * len(column),
        out_specs=[VMEM_SPEC] * 4,
        compiler_params=pltpu.CompilerParams(vmem_limit_bytes=2 << 20),
        cost_estimate=pl.CostEstimate(flops=0, transcendentals=0, bytes_accessed=1<<20),
        name="pick",
    )(owners, pairing, *column)


def merge(blocks_of, scalars, held, got):
    def kernel(scalars_ref, held_ref, got_ref, out_ref):
        chan = lax.axis_index("chan")
        for r, block in enumerate(blocks_of(scalars_ref, chan)):
            same = (chan + block) % 2 == 0
            here, sent, out = (ref if len(ref.shape) == 2 else ref.at[r] for ref in (held_ref, got_ref, out_ref))

            @pl.when(same)
            def _():
                out[...] = white_block(here[...])

            @pl.when(jnp.logical_not(same))
            def _():
                out[...] = white_block(sent[...])

    return pl.pallas_call(
        kernel,
        out_shape=jax.ShapeDtypeStruct(held.shape, bf16),
        in_specs=[SMEM_SPEC, VMEM_SPEC, VMEM_SPEC],
        out_specs=VMEM_SPEC,
        compiler_params=pltpu.CompilerParams(vmem_limit_bytes=4 << 20),
        cost_estimate=pl.CostEstimate(flops=0, transcendentals=0, bytes_accessed=1<<20),
        name="merge",
    )(scalars, held, got)


def shift_kernel(block_ref, out_ref, white_ref, *raw_ref):
    for ref in raw_ref:
        ref[...] = block_ref[...]
    white_ref[...] = white_block(block_ref[...])
    blk, length = block_ref.shape
    lane = lax.broadcasted_iota(jnp.int32, (STEP, length), 1)
    row = lax.broadcasted_iota(jnp.int32, (STEP, length), 0)
    for i in range(blk):
        samples = jnp.broadcast_to(white_ref[i : i + 1, :].astype(f32), (STEP, length))
        moved = pltpu.roll(samples, 0, 1, stride=1, stride_axis=0)
        out_ref[i * STEP : (i + 1) * STEP, :] = jnp.where(lane < row, 0.0, moved).astype(bf16)


def shifted_copies(block, raw=False):
    blk, length = block.shape
    return pl.pallas_call(
        shift_kernel,
        out_shape=[
            jax.ShapeDtypeStruct((blk * STEP, length), bf16),
            jax.ShapeDtypeStruct((blk, length), bf16),
        ]
        + [jax.ShapeDtypeStruct((blk, length), bf16)] * raw,
        in_specs=[VMEM_SPEC],
        out_specs=[VMEM_SPEC] * (2 + raw),
        compiler_params=pltpu.CompilerParams(vmem_limit_bytes=4 << 20),
        cost_estimate=pl.CostEstimate(flops=0, transcendentals=0, bytes_accessed=3<<20),
        name="shifted_copies",
    )(block)


def part_first_kernel(aux_ref, own_ref, out_ref, shifted, own_t):
    blk, length = own_ref.shape
    used = length - CODA_LO
    step = pl.program_id(0)

    @pl.when(step == 0)
    def _():
        own_t[:length, :] = own_ref[...].T
        own_t[length:, :] = jnp.zeros((own_t.shape[0] - length, blk), bf16)
        samples = aux_ref[...][:, :used].astype(f32)
        for b in range(STEP):
            shifted[b * blk : (b + 1) * blk, :] = shift_right(samples, b)

    halves = [
        own_t[pl.ds(pl.multiple_of(CODA_LO + (2 * step + a) * STEP, STEP), used), :] for a in range(2)
    ]
    out_ref[0] = jnp.dot(shifted[...], jnp.concatenate(halves, axis=1), preferred_element_type=f32)


def part_first(aux, own):
    blk, length = own.shape
    used = length - CODA_LO
    steps = CODA // (2 * STEP)
    return pl.pallas_call(
        part_first_kernel,
        out_shape=jax.ShapeDtypeStruct((steps, STEP * blk, 2 * blk), f32),
        grid=(steps,),
        in_specs=[VMEM_SPEC] * 2,
        out_specs=pl.BlockSpec((1, STEP * blk, 2 * blk), lambda step: (step, 0, 0)),
        scratch_shapes=[pltpu.VMEM((STEP * blk, used), bf16), pltpu.VMEM((length + CODA, blk), bf16)],
        compiler_params=pltpu.CompilerParams(vmem_limit_bytes=16 << 20),
        cost_estimate=pl.CostEstimate(
            flops=2 * CODA * blk * blk * used, transcendentals=0, bytes_accessed=4 * CODA * blk * blk
        ),
        name="part_first",
    )(aux, own)


def coda_kernel(windows, start_ref, end_ref, first, *refs):
    aux_ref, own_ref = refs[:windows], refs[windows : 2 * windows]
    out_ref, moved_ref, shifted, own_t, limits, coda, coda_t, acc, rows = refs[2 * windows :]
    blk, length = own_ref[0].shape
    used = length - CODA_LO
    share = out_ref.shape[1]
    steps = share // 2
    pairs = CODA // 2
    scale_two = 1.0 / math.sqrt((windows + 1) * length)
    scale_three = 1.0 / math.sqrt(blk * CODA)
    win = lax.axis_index("win")

    limits[0] = jnp.broadcast_to(start_ref[...], (blk, blk)).T
    limits[1] = jnp.broadcast_to(end_ref[...], (blk, blk)).T
    for w in range(windows):
        own_t[w, :length, :] = own_ref[w][...].T
        own_t[w, length:, :] = jnp.zeros((own_t.shape[1] - length, blk), bf16)
        samples = aux_ref[w][:, :used].astype(f32)
        for b in range(STEP):
            shifted[b * blk : (b + 1) * blk, w * used : (w + 1) * used] = shift_right(samples, b)
    coda[CODA * blk :, :] = jnp.zeros((coda.shape[0] - CODA * blk, blk), bf16)
    coda_t[: (steps - 1) * blk, :] = jnp.zeros(((steps - 1) * blk, 2 * blk), bf16)

    chunk = STEP // 2

    def part(a_pair, limit):
        pieces = []
        for w in range(windows):
            halves = [
                own_t[w, pl.ds(pl.multiple_of(CODA_LO + (2 * a_pair + a) * STEP, STEP), used), :]
                for a in range(2)
            ]
            pieces.append(jnp.concatenate(halves, axis=1))
        weights = jnp.concatenate(pieces, axis=0)
        for b_first in range(0, STEP, chunk):
            rows_here = slice(b_first * blk, (b_first + chunk) * blk)
            result = jnp.dot(shifted[rows_here, :], weights, preferred_element_type=f32)
            result = (result + first[a_pair, rows_here, :]) * scale_two
            for b in range(chunk):
                for a in range(2):
                    lag = (2 * a_pair + a) * STEP + b_first + b
                    tile = result[b * blk : (b + 1) * blk, a * blk : (a + 1) * blk]
                    if limit == 0:
                        tile = jnp.where(lag >= limits[0], tile, 0.0)
                    if limit == 1:
                        tile = jnp.where(lag < limits[1], tile, 0.0)
                    tile = tile.astype(bf16)
                    coda[pl.ds(pl.multiple_of(lag * blk, blk), blk), :] = tile
                    place = pl.multiple_of((lag // 2 + steps - 1) * blk, blk)
                    coda_t[pl.ds(place, blk), (b % 2) * blk : (b % 2 + 1) * blk] = tile.T

    def run(first_step, last_step, limit):
        def body(step, _):
            part(step, limit)
            return 0

        lax.fori_loop(first_step, last_step, body, 0)

    count = CODA // (2 * STEP)
    run(0, count // 4, 0)
    run(count // 4, 3 * count // 4, None)
    run(3 * count // 4, count, 1)

    def accumulate(group, size, blocks, lag_first, total):
        lhs, rhs = [], []
        for q in range(size):
            pair = group * size + q
            row = (pair + steps - blocks) * blk
            lhs.append(coda_t[pl.ds(pl.multiple_of(row, blk), blocks * blk), :])
            top = (2 * pair + lag_first) * blk
            rhs.append(
                jnp.concatenate(
                    [coda[pl.ds(pl.multiple_of(top + b * blk, blk), 2 * blk), :] for b in range(2)], axis=1
                )
            )
        value = jnp.dot(
            jnp.concatenate(lhs, axis=1), jnp.concatenate(rhs, axis=0), preferred_element_type=f32
        )
        acc[(total - blocks) * blk : total * blk, :] += value

    def correlate(lag_first, total, target_ref, size=GROUP):
        acc[: total * blk, :] = jnp.zeros((total * blk, acc.shape[1]), f32)
        peeled = total // size - 1
        for group in range(peeled):
            accumulate(group, size, (group + 1) * size, lag_first, total)

        def whole(group, _):
            accumulate(group, size, total, lag_first, total)
            return 0

        lax.fori_loop(max(peeled, 0), (pairs - lag_first // 2 + size - 1) // size, whole, 0)
        stride = 2 * total + ROW_PAD
        for i in range(total):
            for b in range(2):
                lag = 2 * (total - 1 - i) + b
                rows[pl.ds(lag, blk, stride=stride), :] = (
                    acc[i * blk : (i + 1) * blk, b * blk : (b + 1) * blk] * scale_three
                )
        target_ref[:, : 2 * total, :] = (
            rows[: blk * stride].reshape(blk, stride, blk)[:, : 2 * total].astype(bf16)
        )

    last = lax.axis_size("win") - 1

    @pl.when(win > 0)
    def _():
        correlate(win * share, steps, out_ref)

    kept = share // 2

    @pl.when(win == 0)
    def _():
        correlate(0, kept // 2, out_ref)

    @pl.when(win > last - kept // MOVED)
    def _():
        correlate(kept + MOVED * (last - win), MOVED // 2, moved_ref, 2 * GROUP)


def finish_kernel(count, *refs):
    moved_refs, (_, out_ref, sems) = refs[:count], refs[count:]
    kept = out_ref.shape[1] - MOVED * count

    @pl.when(lax.axis_index("win") == 0)
    def _():
        copies = [
            pltpu.make_async_copy(moved, out_ref.at[:, kept + MOVED * n : kept + MOVED * (n + 1), :], sems.at[n])
            for n, moved in enumerate(moved_refs)
        ]
        for copy in copies:
            copy.start()
        for copy in copies:
            copy.wait()


def finish(moved, three):
    count = len(moved)
    return pl.pallas_call(
        functools.partial(finish_kernel, count),
        out_shape=jax.ShapeDtypeStruct(three.shape, bf16),
        in_specs=[ANY_SPEC] * (count + 1),
        out_specs=ANY_SPEC,
        scratch_shapes=[pltpu.SemaphoreType.DMA((count,))],
        input_output_aliases={count: 0},
        compiler_params=pltpu.CompilerParams(vmem_limit_bytes=1 << 20),
        name="finish",
    )(*moved, three)


def coda_limit(windows, blk, used):
    return (21 << 20) + 2 * STEP * blk * windows * used


def coda_coherence(start, end, first, aux, own, share):
    windows = len(own)
    blk, length = own[0].shape
    used = length - CODA_LO
    steps = share // 2
    return pl.pallas_call(
        functools.partial(coda_kernel, windows),
        out_shape=[
            jax.ShapeDtypeStruct((blk, share, blk), bf16),
            jax.ShapeDtypeStruct((blk, MOVED, blk), bf16),
        ],
        in_specs=[VMEM_SPEC] * (3 + 2 * windows),
        out_specs=[VMEM_SPEC] * 2,
        scratch_shapes=[
            pltpu.VMEM((STEP * blk, windows * used), bf16),
            pltpu.VMEM((windows, length + CODA, blk), bf16),
            pltpu.VMEM((2, blk, blk), jnp.int32),
            pltpu.VMEM(((CODA + 4 * GROUP) * blk, blk), bf16),
            pltpu.VMEM(((CODA // 2 + steps - 1) * blk, 2 * blk), bf16),
            pltpu.VMEM((steps * blk, 2 * blk), f32),
            pltpu.VMEM(((share + ROW_PAD) * blk, blk), f32),
        ],
        compiler_params=pltpu.CompilerParams(vmem_limit_bytes=coda_limit(windows, blk, used)),
        cost_estimate=pl.CostEstimate(
            flops=2 * CODA * blk * blk * (windows * used + blk * share), transcendentals=0, bytes_accessed=16 << 20
        ),
        name="coda_coherence",
    )(start, end, first, *aux, *own)


def transpose_partners(partner_ref, partner_t):
    rounds, blk, length = partner_ref.shape
    for r in range(rounds):
        partner_t[:length, r * blk : (r + 1) * blk] = partner_ref[r].T
    partner_t[length:, :] = jnp.zeros((partner_t.shape[0] - length, rounds * blk), bf16)


def pair_first_kernel(shifted_ref, partner_ref, out_ref, partner_t):
    length = partner_ref.shape[2]
    steps = pl.num_programs(0)
    step = pl.program_id(0)

    @pl.when(step == 0)
    def _():
        transpose_partners(partner_ref, partner_t)

    top = pl.multiple_of((lax.axis_index("win") * steps + step) * STEP, STEP)
    out_ref[0] = jnp.dot(shifted_ref[...], partner_t[pl.ds(top, length), :], preferred_element_type=f32)


def pair_first(shifted, partner, share):
    rounds, blk, length = partner.shape
    steps = share // STEP
    return pl.pallas_call(
        pair_first_kernel,
        out_shape=jax.ShapeDtypeStruct((steps, blk * STEP, rounds * blk), f32),
        grid=(steps,),
        in_specs=[VMEM_SPEC, VMEM_SPEC],
        out_specs=pl.BlockSpec((1, blk * STEP, rounds * blk), lambda step: (step, 0, 0)),
        scratch_shapes=[pltpu.VMEM((length + LAGS, rounds * blk), bf16)],
        compiler_params=pltpu.CompilerParams(vmem_limit_bytes=12 << 20),
        cost_estimate=pl.CostEstimate(
            flops=2 * share * rounds * blk * blk * length,
            transcendentals=0,
            bytes_accessed=4 * share * rounds * blk * blk,
        ),
        name="pair_first",
    )(shifted, partner)


def pair_kernel(windows, first_ref, *refs):
    shifted, partner_ref = refs[:windows], refs[windows : 2 * windows]
    out_ref, partner_t = refs[2 * windows :]
    rounds, blk, length = partner_ref[0].shape
    scale_two = 1.0 / math.sqrt((windows + 1) * length)
    steps = pl.num_programs(0)
    step = pl.program_id(0)

    @pl.when(step == 0)
    def _():
        for w in range(windows):
            transpose_partners(partner_ref[w], partner_t.at[w])

    top = pl.multiple_of((lax.axis_index("win") * steps + step) * STEP, STEP)
    weights = jnp.concatenate([partner_t[w, pl.ds(top, length), :] for w in range(windows)], axis=0)
    half = blk // 2
    for part in range(2):
        rows = slice(part * half * STEP, (part + 1) * half * STEP)
        samples = jnp.concatenate([shifted[w][rows, :] for w in range(windows)], axis=1)
        result = jnp.dot(samples, weights, preferred_element_type=f32)
        result = ((result + first_ref[0, rows, :]) * scale_two).astype(bf16)
        for r in range(rounds):
            out_ref[r, part * half : (part + 1) * half] = result[:, r * blk : (r + 1) * blk].reshape(
                half, STEP, blk
            )


def pair_coherence(first, shifted, partner, share):
    windows = len(shifted)
    rounds, blk, length = partner[0].shape
    steps = share // STEP
    return pl.pallas_call(
        functools.partial(pair_kernel, windows),
        out_shape=jax.ShapeDtypeStruct((rounds, blk, share, blk), bf16),
        grid=(steps,),
        in_specs=[pl.BlockSpec((1,) + first.shape[1:], lambda step: (step, 0, 0))]
        + [VMEM_SPEC] * (2 * windows),
        out_specs=pl.BlockSpec((rounds, blk, STEP, blk), lambda step: (0, 0, step, 0)),
        scratch_shapes=[pltpu.VMEM((windows, length + LAGS, rounds * blk), bf16)],
        compiler_params=pltpu.CompilerParams(vmem_limit_bytes=20 << 20),
        cost_estimate=pl.CostEstimate(
            flops=2 * rounds * share * blk * blk * windows * length, transcendentals=0, bytes_accessed=16 << 20
        ),
        name="pair_coherence",
    )(first, *shifted, *partner)


def per_device(traces, pairing, aux_owners, coda_start, coda_end):
    win_size = lax.axis_size("win")
    chan_size = lax.axis_size("chan")
    rounds = pairing.shape[0]
    pairing = pairing.reshape(-1)
    raw = traces[0]

    def exchange(block, k):
        return lax.ppermute(block, "win", [(i, i ^ k) for i in range(win_size)])

    def cross(block):
        return lax.ppermute(block, "chan", [(i, i ^ 1) for i in range(chan_size)])

    column = [raw] + [
        lax.ppermute(raw, "chan", [(i, (i + 2 * k) % chan_size) for i in range(chan_size)])
        for k in range(1, chan_size // 2)
    ]
    own_rest = [exchange(raw, k) for k in range(1, win_size)]
    first_copies, own_white, column[0] = shifted_copies(raw, True)
    early = [shifted_copies(block) for block in own_rest[:2]]
    first_copies, own_white, early, column = lax.optimization_barrier((first_copies, own_white, early, column))
    aux_sent, aux_held, sent, held = pick(aux_owners, pairing, column)
    aux_sent, sent, own_rest = lax.optimization_barrier((aux_sent, sent, own_rest[2:]))
    shifted = early + [shifted_copies(block) for block in own_rest]
    copies, own_rest = [both[0] for both in shifted], [both[1] for both in shifted]
    aux = merge(lambda ref, chan: [ref[0]], aux_owners, aux_held, cross(aux_sent))
    partners = merge(
        lambda ref, chan: [ref[r * chan_size + chan] for r in range(rounds)], pairing, held, cross(sent)
    )
    aux_rest = [exchange(aux, k) for k in range(1, win_size)]
    pair_begun = pair_first(first_copies, partners, LAGS // win_size)
    part_begun = part_first(aux, own_white)
    partners, aux_rest, pair_begun, part_begun, copies = lax.optimization_barrier(
        (partners, aux_rest, pair_begun, part_begun, copies)
    )
    partner_rest = [exchange(partners, k) for k in range(1, win_size)]
    three, moved = coda_coherence(coda_start, coda_end, part_begun, aux_rest, own_rest, LAGS3 // win_size)
    pair = pair_coherence(pair_begun, copies, partner_rest, LAGS // win_size)
    helpers = LAGS3 // win_size // 2 // MOVED
    moved = [lax.ppermute(moved, "win", [(win_size - 1 - n, 0)]) for n in range(helpers)]
    pair, three, moved = lax.optimization_barrier((pair, three, moved))
    return (pair, finish(moved, three))


def solution(mesh):
    in_specs = (P("win", "chan", None), P(), P(), P(), P())
    out_specs = (P(None, "chan", "win", None), P("chan", "win", None))
    return jax.shard_map(per_device, mesh=mesh, in_specs=in_specs, out_specs=out_specs, check_vma=False)
```
